512 devices in a mesh: dom: 128 (over x, y_hi, z), rel: 4 (over y_lo, core).
Axes of the slice: x: 4, y: 4 (y_hi: 2, y_lo: 2; y = y_hi * 2 + y_lo), z: 16, core: 2. Of those that a mesh axis runs over, the one named last changes fastest.
Arguments:
- emb: float32 [32768, 400], P('dom'), may hold values from -1.2 to 1.2
- emb_state: float32 [32768], P('dom'), may hold values from 0.02 to 2
- rel_weight: float32 [32, 400], P('rel'), may hold values from 0.5 to 1.5
- rel_state: float32 [32], P('rel'), may hold values from 1 to 1000
- swap_mask: int32 [1], replicated, may hold values from 1 to 127
- src_rows: int32 [4, 65536], P('rel', 'dom'), may hold values from 0 to 255
- dst_rows: int32 [4, 65536], P('rel', 'dom'), may hold values from 0 to 255
- tile_rel: int32 [4, 512], P('rel', 'dom'), may hold values from 0 to 7
- live_tiles: int32 [4, 128], P('rel', 'dom'), may hold values from 1 to 4, as said below
- neg_tiles: int32 [4, 1024], P('rel', 'dom'), may hold values from 0 to 1
- bound_rows: int32 [32768], P('dom'), may hold values from 0 to 255
- band_src: int32 [4, 32768], P('rel', 'dom'), may hold values from 0 to 255
- band_dst: int32 [4, 32768], P('rel', 'dom'), may hold values from 0 to 255
- band_rel: int32 [4, 256], P('rel', 'dom'), may hold values from 0 to 7
Outputs:
- emb_new: float32 [32768, 400], P('dom')
- state_new: float32 [32768], P('dom')
- rel_new: float32 [32, 400], P('rel')
The draws below stay inside these ranges and needn't reach their ends.
Inputs may be any that keep to these rules, and one draw needn't show every extreme that they name: `live_tiles`: each entry counts the leading edge tiles of one bucket that hold edges; some relation group and partition has all 4 tiles live in every draw. `swap_mask`: the same plan entry holds for every partition, so pairs are mutual.
All inputs are finite; a program needn't handle non-finite values.
Results may differ from the reference program's by a relative error of at most 0.0029.
Values may be sent and summed in bfloat16 or wider, within the bound.
No kernel may reach another device: no remote copies, remote signals or barrier semaphores. Data moves between devices by JAX's collectives and lax.ppermute only.
A program may use at most 64 MiB of HBM per device.

```python
import math
import jax
import jax.numpy as jnp
from jax import lax

D = 400
TILE = 128
P_ROWS = 256
E_TILES = 4
BAND_TILES = 2
NEG_TILES = 8
BND = 128
RELS_DEV = 8
ENT = 32768
RELS = 32
E_ROWS = 512
BAND_ROWS = 256
NEG = 1024
P_TILES = 2
N_DOM = 128
N_REL = 4


def draw_live_tiles(key, part):
    base = jax.random.fold_in(key, 11)
    first, second = jax.random.split(base)
    counts = jax.random.randint(first, (N_REL * N_DOM,), 1, E_TILES + 1)
    place = jax.random.randint(second, (), 0, N_REL * N_DOM)
    counts = jnp.where(jnp.arange(N_REL * N_DOM) == place, E_TILES, counts)
    return counts.reshape(N_REL, N_DOM).astype(jnp.int32)


def draw_rel_state(key, part):
    base = jax.random.fold_in(key, 23)
    values = jnp.exp(jax.random.uniform(base, (RELS,), jnp.float32, 0.0, 6.9))
    return values.astype(jnp.float32)


def set_ends(values, own_key, smallest, largest):
    spot = [jax.random.randint(jax.random.fold_in(own_key, axis), (), 0, length) for axis, length in enumerate(values.shape)]
    longest = values.shape.index(max(values.shape))
    beside = spot[:longest] + [(spot[longest] + 1) % values.shape[longest]] + spot[longest + 1:]
    return values.at[tuple(spot)].set(smallest).at[tuple(beside)].set(largest)


def level_of(rng, dims, cuts, low, top_value):
    gain, own = 1.0, jax.random.fold_in(rng, 6)
    for position, shards_of in cuts:
        draws = jnp.exp(jax.random.uniform(jax.random.fold_in(own, position), (shards_of,), jnp.float32, low / len(cuts), top_value / len(cuts)))
        gain = gain * jnp.repeat(draws, dims[position] // shards_of).reshape([-1 if axis == position else 1 for axis in range(len(dims))])
    return gain


def scatter_about(key, shape, scale, reach, cuts=(), dtype=jnp.bfloat16):
    factor_of = level_of(key, shape, cuts, -0.22, 0.18) if cuts else 1.0
    result = jax.random.normal(key, shape, jnp.float32) * scale * factor_of
    return jnp.minimum(jnp.maximum(result, -reach), reach).astype(dtype)


def setup_inputs(seed: int = 0) -> dict:
    streams_of = jax.random.split(jax.random.key(seed), 15)
    return {
        "emb": scatter_about(streams_of[0], (ENT, D), 0.2, 1.2, ((0, 128),), jnp.float32),
        "emb_state": jnp.clip(jnp.exp(math.log(2.0) - 4.6051702 * jax.random.uniform(streams_of[1], (ENT,), jnp.float32) ** level_of(streams_of[1], (ENT,), ((0, 128),), -0.2, 0.2)), 0.02, 2.0),
        "rel_weight": jnp.clip(1.0 + 0.1 * jax.random.normal(streams_of[2], (RELS, D), jnp.float32), 0.5, 1.5),
        "rel_state": draw_rel_state(jax.random.fold_in(streams_of[14], 71), 0),
        "swap_mask": jax.random.randint(streams_of[4], (1,), 1, N_DOM).astype(jnp.int32),
        "src_rows": set_ends(jax.random.randint(streams_of[5], (N_REL, N_DOM * E_ROWS), 0, P_ROWS), jax.random.fold_in(streams_of[5], 1), 0, P_ROWS - 1).astype(jnp.int32),
        "dst_rows": set_ends(jax.random.randint(streams_of[6], (N_REL, N_DOM * E_ROWS), 0, P_ROWS), jax.random.fold_in(streams_of[6], 1), 0, P_ROWS - 1).astype(jnp.int32),
        "tile_rel": set_ends(jax.random.randint(streams_of[7], (N_REL, N_DOM * E_TILES), 0, RELS_DEV), jax.random.fold_in(streams_of[7], 1), 0, RELS_DEV - 1).astype(jnp.int32),
        "live_tiles": draw_live_tiles(jax.random.fold_in(streams_of[14], 71), 0),
        "neg_tiles": set_ends(jax.random.randint(streams_of[9], (N_REL, N_DOM * NEG_TILES), 0, P_TILES), jax.random.fold_in(streams_of[9], 1), 0, P_TILES - 1).astype(jnp.int32),
        "bound_rows": set_ends(jax.random.randint(streams_of[10], (N_DOM * 2 * BND,), 0, P_ROWS), jax.random.fold_in(streams_of[10], 1), 0, P_ROWS - 1).astype(jnp.int32),
        "band_src": set_ends(jax.random.randint(streams_of[11], (N_REL, N_DOM * BAND_ROWS), 0, P_ROWS), jax.random.fold_in(streams_of[11], 1), 0, P_ROWS - 1).astype(jnp.int32),
        "band_dst": set_ends(jax.random.randint(streams_of[12], (N_REL, N_DOM * BAND_ROWS), 0, 2 * BND), jax.random.fold_in(streams_of[12], 1), 0, (2 * BND) - 1).astype(jnp.int32),
        "band_rel": set_ends(jax.random.randint(streams_of[13], (N_REL, N_DOM * BAND_TILES), 0, RELS_DEV), jax.random.fold_in(streams_of[13], 1), 0, RELS_DEV - 1).astype(jnp.int32),
    }


def edge_terms(q, target, negs, valid):
    pos = lax.optimization_barrier(jnp.sum(q.astype(jnp.float32) * target.astype(jnp.float32), axis=1))
    neg = jnp.einsum('ed,nd->en', q, negs, preferred_element_type=jnp.float32)
    dpos = -jax.nn.sigmoid(-pos) * valid
    dneg = (jax.nn.sigmoid(neg) * (valid / negs.shape[0])[:, None]).astype(jnp.bfloat16)
    dq = dpos[:, None] * target.astype(jnp.float32) + jnp.einsum('en,nd->ed', dneg, negs, preferred_element_type=jnp.float32)
    dtarget = dpos[:, None] * q.astype(jnp.float32)
    dnegs = jnp.einsum('en,ed->nd', dneg, q, preferred_element_type=jnp.float32)
    return (dq, dtarget, dnegs)

def reference(emb, emb_state, rel_weight, rel_state, swap_mask, src_rows, dst_rows, tile_rel, live_tiles, neg_tiles, bound_rows, band_src, band_dst, band_rel):
    blocks = emb.reshape(N_DOM, P_ROWS, D)
    bounds = bound_rows.reshape(N_DOM, 2 * BND)
    mask = swap_mask[0].astype(jnp.int32)
    tile_of_edge = (jnp.arange(E_ROWS) // TILE).astype(jnp.int32)

    def one_device(index, carry):
        grads, rel_grads = carry
        index = jnp.asarray(index).astype(jnp.int32)
        dom_index = (index // N_REL).astype(jnp.int32)
        rel_index = (index % N_REL).astype(jnp.int32)
        own = blocks[dom_index]
        partner = jnp.bitwise_xor(dom_index, mask).astype(jnp.int32)
        far = blocks[partner].astype(jnp.bfloat16)
        lower = jnp.maximum(dom_index - 1, 0).astype(jnp.int32)
        upper = jnp.minimum(dom_index + 1, N_DOM - 1).astype(jnp.int32)
        has_lower = (dom_index > 0).astype(jnp.float32)
        has_upper = (dom_index < N_DOM - 1).astype(jnp.float32)
        lower_list = bounds[lower][BND:]
        upper_list = bounds[upper][:BND]
        near = jnp.concatenate([blocks[lower][lower_list] * has_lower, blocks[upper][upper_list] * has_upper], axis=0).astype(jnp.bfloat16)
        weights = lax.dynamic_slice_in_dim(rel_weight, rel_index * RELS_DEV, RELS_DEV, 0)
        src = lax.dynamic_slice(src_rows, (rel_index, dom_index * E_ROWS), (1, E_ROWS))[0]
        dst = lax.dynamic_slice(dst_rows, (rel_index, dom_index * E_ROWS), (1, E_ROWS))[0]
        rel_tiles = lax.dynamic_slice(tile_rel, (rel_index, dom_index * E_TILES), (1, E_TILES))[0]
        neg_ids = lax.dynamic_slice(neg_tiles, (rel_index, dom_index * NEG_TILES), (1, NEG_TILES))[0]
        bsrc = lax.dynamic_slice(band_src, (rel_index, dom_index * BAND_ROWS), (1, BAND_ROWS))[0]
        bdst = lax.dynamic_slice(band_dst, (rel_index, dom_index * BAND_ROWS), (1, BAND_ROWS))[0]
        brel_tiles = lax.dynamic_slice(band_rel, (rel_index, dom_index * BAND_TILES), (1, BAND_TILES))[0]
        live = live_tiles[rel_index, dom_index]
        valid = (tile_of_edge < live).astype(jnp.float32)
        rel_edge = jnp.repeat(rel_tiles, TILE)
        rel_band = jnp.repeat(brel_tiles, TILE)
        rel_all = jnp.concatenate([rel_edge, rel_band])
        src_all = jnp.concatenate([src, bsrc])
        w_all = weights[rel_all]
        rows_all = own[src_all]
        q = (rows_all * w_all).astype(jnp.bfloat16)
        negs = far.reshape(P_TILES, TILE, D)[neg_ids].reshape(NEG, D)
        target = jnp.concatenate([far[dst], near[bdst]], axis=0)
        valid_all = jnp.concatenate([valid, jnp.ones((BAND_ROWS,), jnp.float32)])
        dq, dtarget, dnegs = edge_terms(q, target, negs, valid_all)
        own_grad = jnp.zeros((P_ROWS, D), jnp.float32).at[src_all].add(dq * w_all)
        rel_term = jnp.zeros((RELS_DEV, D), jnp.float32).at[rel_all].add(dq * rows_all)
        far_grad = jnp.zeros((P_ROWS, D), jnp.float32).at[dst].add(dtarget[:E_ROWS])
        far_grad = far_grad.reshape(P_TILES, TILE, D).at[neg_ids].add(dnegs.reshape(NEG_TILES, TILE, D)).reshape(P_ROWS, D)
        near_grad = jnp.zeros((2 * BND, D), jnp.float32).at[bdst].add(dtarget[E_ROWS:])
        grads = grads.at[dom_index].add(own_grad)
        grads = grads.at[partner].add(far_grad)
        grads = grads.at[lower, lower_list].add(near_grad[:BND] * has_lower)
        grads = grads.at[upper, upper_list].add(near_grad[BND:] * has_upper)
        rel_grads = rel_grads.at[rel_index].add(rel_term)
        return (grads, rel_grads)
    start = (jnp.zeros((N_DOM, P_ROWS, D), jnp.float32), jnp.zeros((N_REL, RELS_DEV, D), jnp.float32))
    grads, rel_grads = lax.fori_loop(0, N_DOM * N_REL, one_device, start)
    full_grad = grads.reshape(ENT, D)
    state_new = emb_state + lax.optimization_barrier(jnp.mean(full_grad * full_grad, axis=1))
    emb_new = emb - 0.25 * full_grad / jnp.sqrt(state_new)[:, None]
    rel_grad = rel_grads.reshape(RELS, D)
    rel_new = rel_weight - 0.25 * rel_grad / jnp.sqrt(rel_state + lax.optimization_barrier(jnp.mean(rel_grad * rel_grad, axis=1)))[:, None]
    return (emb_new, state_new, rel_new)
```

```python
import jax
import jax.numpy as jnp
from jax import lax
from jax.experimental import pallas as pl
from jax.experimental.pallas import tpu as pltpu
from jax.sharding import Mesh
from jax.sharding import PartitionSpec as P

step_rate = 0.25

D = 400
TILE = 128
ROWS = 256
BND = 128
E_ROWS = 512
B_ROWS = 256
A_ROWS = E_ROWS + B_ROWS
E_TILES = E_ROWS // TILE
B_TILES = B_ROWS // TILE
A_TILES = E_TILES + B_TILES
N_REL = 4
PART = ROWS // N_REL
RELS = 8
NEG_TILES = 8
NEG = NEG_TILES * TILE

BF = jnp.bfloat16
F32 = jnp.float32
DOM = ("x", "yh", "z")
Z = 16
XY = 8


def vmem():
    return pl.BlockSpec(memory_space=pltpu.VMEM)


def smem():
    return pl.BlockSpec(memory_space=pltpu.SMEM)


def call(kernel, ins, outs, *args):
    return pl.pallas_call(
        kernel,
        in_specs=[smem() if kind == "s" else vmem() for kind in ins],
        out_specs=[vmem() for _ in outs],
        out_shape=[jax.ShapeDtypeStruct(shape, dtype) for shape, dtype in outs],
    )(*args)


def mm(a, b, dims):
    return lax.dot_general(a, b, (dims, ((), ())), preferred_element_type=F32)


def two(values):
    high = values.astype(BF)
    return high, (values - high.astype(F32)).astype(BF)


def onehot_t(rows, ids):
    return lax.broadcasted_iota(jnp.int32, (rows, ids.shape[1]), 0) == ids


def start_kernel(rel_ref, emb_ref, bound_ref, part_ref, low_ref, high_ref):
    first = pl.multiple_of(rel_ref[0] * PART, PART)
    part_ref[...] = emb_ref[pl.ds(first, PART), :].astype(BF)
    pick = onehot_t(ROWS, bound_ref[...]).astype(F32).astype(BF)
    rim = mm(pick, emb_ref[...].astype(BF), ((0,), (0,))).astype(BF)
    low_ref[...] = rim[:BND]
    high_ref[...] = rim[BND:]


def source_kernel(
    tile_ref, band_ref, emb_ref, rel_ref, src_ref, bsrc_ref, bdst_ref, low_ref, high_ref,
    q_ref, rows_ref, dqb_ref, glow_ref, ghigh_ref,
):
    emb_high, emb_low = two(emb_ref[...])
    for ids_ref, first, count, tiles in (
        (bsrc_ref, E_ROWS, B_ROWS, band_ref),
        (src_ref, 0, E_ROWS, tile_ref),
    ):
        pick = onehot_t(ROWS, ids_ref[...]).astype(F32).astype(BF)
        rows = mm(pick, emb_high, ((0,), (0,))) + mm(pick, emb_low, ((0,), (0,)))
        rows_ref[first : first + count, :] = rows
        for t in range(count // TILE):
            w = rel_ref[pl.ds(tiles[0, t], 1), :]
            q_ref[first + t * TILE : first + (t + 1) * TILE, :] = (
                rows[t * TILE : (t + 1) * TILE] * w
            ).astype(BF)
    qb = q_ref[E_ROWS:, :]
    near = jnp.concatenate([low_ref[...], high_ref[...]], axis=0)
    scores = mm(near, qb, ((1,), (1,)))
    hit = onehot_t(2 * BND, bdst_ref[...])
    pos = jnp.sum(jnp.where(hit, scores, 0.0), axis=0, keepdims=True)
    dpos = -jax.nn.sigmoid(-pos)
    high, low = two(jnp.where(hit, dpos, 0.0))
    dqb_ref[...] = mm(high, near, ((0,), (0,))) + mm(low, near, ((0,), (0,)))
    grad = (mm(high, qb, ((1,), (0,))) + mm(low, qb, ((1,), (0,)))).astype(BF)
    glow_ref[...] = grad[:BND]
    ghigh_ref[...] = grad[BND:]


def bucket_kernel(
    tile_ref, band_ref, live_ref, neg_ref, far_ref, q_ref, rows_ref, dqb_ref, rel_ref,
    src_ref, bsrc_ref, dst_ref, bound_ref, rlow_ref, rhigh_ref,
    send_ref, gw_ref,
):
    far = far_ref[...]
    q = q_ref[...]
    scores = mm(far, q, ((1,), (1,)))
    edge = lax.broadcasted_iota(jnp.int32, (1, A_ROWS), 1)
    valid = jnp.where((edge < live_ref[0, 0] * TILE) | (edge >= E_ROWS), 1.0, 0.0)
    hit = onehot_t(ROWS, dst_ref[...])
    pos = jnp.sum(jnp.where(hit, scores[:, :E_ROWS], 0.0), axis=0, keepdims=True)
    dpos = -jax.nn.sigmoid(-pos) * valid[:, :E_ROWS]
    second = neg_ref[0, 0]
    for t in range(1, NEG_TILES):
        second = second + neg_ref[0, t]
    second = second.astype(F32)
    counts = jnp.where(
        lax.broadcasted_iota(jnp.int32, (ROWS, 1), 0) < TILE, NEG_TILES - second, second
    )
    dneg = (jax.nn.sigmoid(scores) * (valid / NEG)).astype(BF).astype(F32) * counts
    coef = jnp.concatenate(
        [dneg[:, :E_ROWS] + jnp.where(hit, dpos, 0.0), dneg[:, E_ROWS:]], axis=1
    )
    high, low = two(coef)
    far_grad = mm(high, q, ((1,), (0,))) + mm(low, q, ((1,), (0,)))
    dq = mm(high, far, ((0,), (0,))) + mm(low, far, ((0,), (0,)))
    gw = jnp.zeros((RELS, D), F32)
    row8 = lax.broadcasted_iota(jnp.int32, (RELS, 1), 0)
    parts = []
    for t in range(A_TILES):
        ident = tile_ref[0, t] if t < E_TILES else band_ref[0, t - E_TILES]
        piece = dq[t * TILE : (t + 1) * TILE]
        if t >= E_TILES:
            first = (t - E_TILES) * TILE
            piece = piece + dqb_ref[first : first + TILE, :]
        total = jnp.sum(piece * rows_ref[t * TILE : (t + 1) * TILE, :], axis=0, keepdims=True)
        gw = gw + jnp.where(row8 == ident, total, 0.0)
        parts.append(piece * rel_ref[pl.ds(ident, 1), :])
    gw_ref[...] = gw
    step_high, step_low = two(jnp.concatenate(parts, axis=0))
    pick = jnp.concatenate(
        [
            onehot_t(ROWS, src_ref[...]).astype(F32).astype(BF),
            onehot_t(ROWS, bsrc_ref[...]).astype(F32).astype(BF),
        ],
        axis=1,
    )
    own = mm(pick, step_high, ((1,), (0,))) + mm(pick, step_low, ((1,), (0,)))
    back = jnp.concatenate([rlow_ref[...], rhigh_ref[...]], axis=0)
    own = own + mm(onehot_t(ROWS, bound_ref[...]).astype(F32).astype(BF), back, ((1,), (0,)))
    for r in range(N_REL):
        send_ref[r, :PART, :] = far_grad[r * PART : (r + 1) * PART].astype(BF)
        send_ref[r, PART:, :] = own[r * PART : (r + 1) * PART].astype(BF)


def swap(values, mask):
    def along(axes, size, part, moved):
        def branch(number):
            def run(block):
                if number == 0:
                    return block
                return lax.ppermute(block, axes, [(i, i ^ number) for i in range(size)])

            return run

        return lax.switch(part, [branch(number) for number in range(size)], moved)

    values = along(("x", "yh"), XY, mask // Z, values)
    return along("z", Z, mask % Z, values)


def body(
    emb, emb_state, rel_weight, rel_state, swap_mask, src_rows, dst_rows, tile_rel, live_tiles,
    neg_tiles, bound_rows, band_src, band_dst, band_rel,
):
    mask = swap_mask[0]
    bound = bound_rows.reshape(1, 2 * BND)
    rel_index = lax.axis_index("rel").reshape(1)
    count = lax.axis_size(DOM)
    up = [(i, i + 1) for i in range(count - 1)]
    down = [(i + 1, i) for i in range(count - 1)]
    part, rim_low, rim_high = call(
        start_kernel,
        "svv",
        [((PART, D), BF), ((BND, D), BF), ((BND, D), BF)],
        rel_index, emb, bound,
    )
    near_low = lax.ppermute(rim_high, DOM, up)
    near_high = lax.ppermute(rim_low, DOM, down)
    q, rows, dq_band, grad_low, grad_high = call(
        source_kernel,
        "ssvvvvvvv",
        [((A_ROWS, D), BF), ((A_ROWS, D), F32), ((B_ROWS, D), F32), ((BND, D), BF), ((BND, D), BF)],
        tile_rel, band_rel, emb, rel_weight, src_rows, band_src, band_dst, near_low, near_high,
    )
    ret_low = lax.ppermute(grad_high, DOM, up)
    ret_high = lax.ppermute(grad_low, DOM, down)
    far = lax.all_gather(swap(part, mask), "rel", axis=0, tiled=True)
    send, gw = call(
        bucket_kernel,
        "ssssvvvvvvvvvvv",
        [((N_REL, 2 * PART, D), BF), ((RELS, D), F32)],
        tile_rel, band_rel, live_tiles, neg_tiles, far, q, rows, dq_band, rel_weight,
        src_rows, band_src, dst_rows, bound, ret_low, ret_high,
    )
    got = lax.all_to_all(send, "rel", split_axis=0, concat_axis=0, tiled=True)
    summed = jnp.sum(got.astype(F32), axis=0)
    back = swap(summed[:PART].astype(BF), mask)
    grad_part = (summed[PART:] + back.astype(F32)).astype(BF)
    grad = lax.all_gather(grad_part, "rel", axis=0, tiled=True).astype(F32)
    state_new = emb_state + jnp.mean(grad * grad, axis=1)
    emb_new = emb - step_rate * grad / jnp.sqrt(state_new)[:, None]

    for axes, size in (("z", Z), (("x", "yh"), XY)):
        copies = jnp.broadcast_to(gw.astype(BF)[None], (size, RELS, D))
        gw = jnp.sum(
            lax.all_to_all(copies, axes, split_axis=0, concat_axis=0, tiled=True).astype(F32), axis=0
        )
    rel_new = rel_weight - step_rate * gw / jnp.sqrt(rel_state + jnp.mean(gw * gw, axis=1))[:, None]
    return (emb_new, state_new, rel_new)


def solution(mesh):
    fine = Mesh(mesh.devices.reshape(4, 2, Z, N_REL), ("x", "yh", "z", "rel"))
    in_specs = (
        P(DOM, None),
        P(DOM),
        P("rel", None),
        P("rel"),
        P(),
        P("rel", DOM),
        P("rel", DOM),
        P("rel", DOM),
        P("rel", DOM),
        P("rel", DOM),
        P(DOM),
        P("rel", DOM),
        P("rel", DOM),
        P("rel", DOM),
    )
    out_specs = (P(DOM, None), P(DOM), P("rel", None))
    return jax.shard_map(body, mesh=fine, in_specs=in_specs, out_specs=out_specs, check_vma=False)
```

```python
import jax
import jax.numpy as jnp
from jax import lax
from jax.experimental import pallas as pl
from jax.experimental.pallas import tpu as pltpu
from jax.sharding import Mesh
from jax.sharding import PartitionSpec as P

step_rate = 0.25

D = 400
TILE = 128
ROWS = 256
BND = 128
E_ROWS = 512
B_ROWS = 256
A_ROWS = E_ROWS + B_ROWS
E_TILES = E_ROWS // TILE
B_TILES = B_ROWS // TILE
A_TILES = E_TILES + B_TILES
N_REL = 4
HALF = ROWS // 2
PART = ROWS // N_REL
INFO = 8
SENT = PART + INFO
RELS = 8
NEG_TILES = 8
NEG = NEG_TILES * TILE
RIM = BND + B_ROWS + INFO

BF = jnp.bfloat16
F32 = jnp.float32
DOM = ("x", "yh", "z")
Z = 16
XY = 8


def vmem():
    return pl.BlockSpec(memory_space=pltpu.VMEM)


def smem():
    return pl.BlockSpec(memory_space=pltpu.SMEM)


def call(kernel, ins, outs, *args):
    return pl.pallas_call(
        kernel,
        in_specs=[smem() if kind == "s" else vmem() for kind in ins],
        out_specs=[vmem() for _ in outs],
        out_shape=[jax.ShapeDtypeStruct(shape, dtype) for shape, dtype in outs],
    )(*args)


def mm(a, b, dims):
    return lax.dot_general(a, b, (dims, ((), ())), preferred_element_type=F32)


NN = ((1,), (0,))
NT = ((1,), (1,))
TN = ((0,), (0,))


def two(values):
    high = values.astype(BF)
    return high, (values - high.astype(F32)).astype(BF)


def mm_two(a, b, dims):
    high, low = two(a)
    return mm(high, b, dims) + mm(low, b, dims)


def hits(rows, ids):
    return lax.broadcasted_iota(jnp.int32, (rows, ids.shape[1]), 0) == ids


def picks(rows, ids):
    return hits(rows, ids).astype(F32).astype(BF)


def row_of(lists):
    row = lax.broadcasted_iota(jnp.int32, (INFO, D), 0)
    block = jnp.zeros((INFO, D), F32)
    for k, values in enumerate(lists):
        if values.shape[1] < D:
            values = jnp.concatenate([values, jnp.zeros((1, D - values.shape[1]), F32)], axis=1)
        block = jnp.where(row == k, values, block)
    return block.astype(BF)


def start_kernel(
    rel_ref, tile_ref, band_ref, live_ref, neg_ref, embt_ref, relw_ref, src_ref, dst_ref, bsrc_ref,
    bdst_ref, bound_ref,
    emb_ref, part_ref, up_ref, down_ref, brows_ref,
):
    emb = embt_ref[...].T
    emb_ref[...] = emb
    emb_high, emb_low = two(emb)
    first = pl.multiple_of(rel_ref[0] * PART, PART)
    part_ref[:PART, :] = emb_ref[pl.ds(first, PART), :].astype(BF)
    lane = lax.broadcasted_iota(jnp.int32, (1, D), 1)
    second = neg_ref[0, 0]
    for t in range(1, NEG_TILES):
        second = second + neg_ref[0, t]
    numbers = [tile_ref[0, t] for t in range(E_TILES)] + [band_ref[0, t] for t in range(B_TILES)]
    numbers += [live_ref[0, 0], second]
    scalars = jnp.zeros((1, D), F32)
    for k, number in enumerate(numbers):
        scalars = jnp.where(lane == k, number.astype(F32), scalars)
    part_ref[PART:, :] = row_of(
        [
            src_ref[:, :256].astype(F32),
            src_ref[:, 256:].astype(F32),
            dst_ref[:, :256].astype(F32),
            dst_ref[:, 256:].astype(F32),
            bsrc_ref[...].astype(F32),
            scalars,
        ]
    )
    rim = mm(picks(ROWS, bound_ref[...]), emb_high, TN).astype(BF)
    up_ref[:BND, :] = rim[BND:]
    down_ref[:BND, :] = rim[:BND]
    pick = picks(ROWS, bsrc_ref[...])
    rows = mm(pick, emb_high, TN) + mm(pick, emb_low, TN)
    brows_ref[...] = rows
    for t in range(B_TILES):
        q = (rows[t * TILE : (t + 1) * TILE] * relw_ref[pl.ds(band_ref[0, t], 1), :]).astype(BF)
        up_ref[BND + t * TILE : BND + (t + 1) * TILE, :] = q
        down_ref[BND + t * TILE : BND + (t + 1) * TILE, :] = q
    info = row_of([bdst_ref[...].astype(F32)])
    up_ref[BND + B_ROWS :, :] = info
    down_ref[BND + B_ROWS :, :] = info


def source_kernel(
    tile_ref, emb_ref, relw_ref, src_ref, bdst_ref, bound_ref, sent_ref, own_up_ref, own_down_ref,
    low_ref, high_ref,
    q_ref, rows_ref, dqb_ref, back_ref,
):
    emb_high, emb_low = two(emb_ref[...])
    pick = picks(ROWS, src_ref[...])
    rows = mm(pick, emb_high, TN) + mm(pick, emb_low, TN)
    rows_ref[...] = rows
    for t in range(E_TILES):
        at = slice(t * TILE, (t + 1) * TILE)
        q_ref[at, :] = (rows[at] * relw_ref[pl.ds(tile_ref[0, t], 1), :]).astype(BF)
    qb = own_up_ref[BND : BND + B_ROWS, :]
    q_ref[E_ROWS:, :] = qb
    near = jnp.concatenate([low_ref[:BND, :], high_ref[:BND, :]], axis=0)
    hit = hits(2 * BND, bdst_ref[...])
    pos = jnp.sum(jnp.where(hit, mm(near, qb, NT), 0.0), axis=0, keepdims=True)
    dqb_ref[...] = mm_two(jnp.where(hit, -jax.nn.sigmoid(-pos), 0.0), near, TN)
    grads = []
    for got_ref, mine_ref, shift in ((low_ref, own_down_ref, BND), (high_ref, own_up_ref, 0)):
        qn = got_ref[BND : BND + B_ROWS, :]
        ids = got_ref[BND + B_ROWS :, :].astype(F32)[:1, :B_ROWS].astype(jnp.int32) - shift
        hit = hits(BND, ids)
        pos = jnp.sum(jnp.where(hit, mm(mine_ref[:BND, :], qn, NT), 0.0), axis=0, keepdims=True)
        grads.append(mm_two(jnp.where(hit, -jax.nn.sigmoid(-pos), 0.0), qn, NN))
    high, low = two(jnp.concatenate(grads, axis=0))
    pick = picks(ROWS, bound_ref[...])
    back_ref[...] = mm(pick, high, NN) + mm(pick, low, NN)


def coefficients(scores, dst, live, second):
    edge = lax.broadcasted_iota(jnp.int32, (1, A_ROWS), 1)
    valid = jnp.where((edge < live * TILE) | (edge >= E_ROWS), 1.0, 0.0)
    hit = hits(ROWS, dst)
    pos = jnp.sum(jnp.where(hit, scores[:, :E_ROWS], 0.0), axis=0, keepdims=True)
    dpos = -jax.nn.sigmoid(-pos) * valid[:, :E_ROWS]
    counts = jnp.where(
        lax.broadcasted_iota(jnp.int32, (ROWS, 1), 0) < TILE, NEG_TILES - second, second
    )
    dneg = (jax.nn.sigmoid(scores) * (valid / NEG)).astype(BF).astype(F32) * counts
    return jnp.concatenate(
        [dneg[:, :E_ROWS] + jnp.where(hit, dpos, 0.0), dneg[:, E_ROWS:]], axis=1
    )


def far_rows(far_ref):
    return jnp.concatenate(
        [far_ref[r * SENT : r * SENT + PART, :] for r in range(N_REL)], axis=0
    )


def relation_kernel(
    tile_ref, band_ref, live_ref, neg_ref, far_ref, q_ref, rows_ref, brows_ref, dqb_ref, relw_ref,
    src_ref, bsrc_ref, dst_ref, back_ref,
    gw_ref, local_ref,
):
    far = far_rows(far_ref)
    second = neg_ref[0, 0]
    for t in range(1, NEG_TILES):
        second = second + neg_ref[0, t]
    scores = mm(far, q_ref[...], NT)
    coef = coefficients(scores, dst_ref[...], live_ref[0, 0], second.astype(F32))
    dq = mm_two(coef, far, TN)
    gw = jnp.zeros((RELS, D), F32)
    row8 = lax.broadcasted_iota(jnp.int32, (RELS, 1), 0)
    steps = []
    for t in range(A_TILES):
        piece = dq[t * TILE : (t + 1) * TILE]
        if t < E_TILES:
            ident = tile_ref[0, t]
            rows = rows_ref[t * TILE : (t + 1) * TILE, :]
        else:
            at = slice((t - E_TILES) * TILE, (t - E_TILES + 1) * TILE)
            ident = band_ref[0, t - E_TILES]
            rows = brows_ref[at, :]
            piece = piece + dqb_ref[at, :]
        gw = gw + jnp.where(row8 == ident, jnp.sum(piece * rows, axis=0, keepdims=True), 0.0)
        steps.append(piece * relw_ref[pl.ds(ident, 1), :])
    for k in range(Z):
        gw_ref[k, :, :] = gw.astype(BF)
    high, low = two(jnp.concatenate(steps, axis=0))
    pick = jnp.concatenate([picks(ROWS, src_ref[...]), picks(ROWS, bsrc_ref[...])], axis=1)
    local_ref[...] = back_ref[...] + mm(pick, high, NN) + mm(pick, low, NN)


def partner_kernel(
    core_ref, far_ref, got_ref, emb_ref, relw_ref, local_ref,
    keep_ref, give_ref, total_ref,
):
    far = far_rows(far_ref)
    info = got_ref[PART:, :].astype(F32)
    src = jnp.concatenate([info[0:1, :256], info[1:2, :256], info[4:5, :256]], axis=1)
    dst = jnp.concatenate([info[2:3, :256], info[3:4, :256]], axis=1).astype(jnp.int32)
    rows = mm(picks(ROWS, src.astype(jnp.int32)), far, TN)
    row8 = lax.broadcasted_iota(jnp.int32, (RELS, 1), 0)
    parts = []
    for t in range(A_TILES):
        chosen = row8 == info[5:6, t : t + 1].astype(jnp.int32)
        w = jnp.sum(jnp.where(chosen, relw_ref[...], 0.0), axis=0, keepdims=True)
        parts.append((rows[t * TILE : (t + 1) * TILE] * w).astype(BF))
    q = jnp.concatenate(parts, axis=0)
    scores = mm(emb_ref[...].astype(BF), q, NT)
    coef = coefficients(
        scores, dst, info[5:6, A_TILES : A_TILES + 1].astype(jnp.int32), info[5:6, A_TILES + 1 : A_TILES + 2]
    )
    total_ref[...] = local_ref[...] + mm_two(coef, q, NN)
    mine = pl.multiple_of(core_ref[0] * HALF, HALF)
    other = pl.multiple_of((1 - core_ref[0]) * HALF, HALF)
    keep_ref[...] = total_ref[pl.ds(mine, HALF), :]
    give_ref[...] = total_ref[pl.ds(other, HALF), :].astype(BF)


def final_kernel(core_ref, mine_ref, other_ref, embt_ref, state_ref, new_ref, fresh_ref):
    first = core_ref[0] == 0
    mine, other = mine_ref[...].astype(F32), other_ref[...].astype(F32)
    grad = jnp.concatenate(
        [jnp.where(first, mine, other), jnp.where(first, other, mine)], axis=0
    ).T
    fresh = state_ref[...] + jnp.sum(grad * grad, axis=0, keepdims=True) / D
    fresh_ref[...] = fresh
    new_ref[...] = embt_ref[...] - step_rate * grad / jnp.sqrt(fresh)


def swap(values, mask):
    def along(axes, size, part, moved):
        def branch(number):
            def run(block):
                if number == 0:
                    return block
                return lax.ppermute(block, axes, [(i, i ^ number) for i in range(size)])

            return run

        return lax.switch(part, [branch(number) for number in range(size)], moved)

    values = along(("x", "yh"), XY, lax.shift_right_logical(mask, 4), values)
    return along("z", Z, lax.bitwise_and(mask, 15), values)


def trade(values, bit):
    return lax.ppermute(values, "rel", [(i, i ^ bit) for i in range(N_REL)])


def body(
    emb, emb_state, rel_weight, rel_state, swap_mask, src_rows, dst_rows, tile_rel, live_tiles,
    neg_tiles, bound_rows, band_src, band_dst, band_rel,
):
    mask = swap_mask[0]
    bound = bound_rows.reshape(1, 2 * BND)
    rel_index = lax.axis_index("rel").astype(jnp.int32)
    core = lax.bitwise_and(rel_index, 1).reshape(1)
    count = lax.axis_size(DOM)
    part_shape, rim_shape = (SENT, D), (RIM, D)
    emb_rows, part, to_up, to_down, band_rows = call(
        start_kernel,
        "sssssvvvvvvv",
        [((ROWS, D), F32), (part_shape, BF), (rim_shape, BF), (rim_shape, BF), ((B_ROWS, D), F32)],
        rel_index.reshape(1), tile_rel, band_rel, live_tiles, neg_tiles, emb.T, rel_weight, src_rows,
        dst_rows, band_src, band_dst, bound,
    )
    from_low = lax.ppermute(to_up, DOM, [(i, i + 1) for i in range(count - 1)])
    from_high = lax.ppermute(to_down, DOM, [(i + 1, i) for i in range(count - 1)])
    got = swap(part, mask)
    far = lax.all_gather(got, "rel", axis=0, tiled=True)
    q, rows, dq_band, back = call(
        source_kernel,
        "svvvvvvvvvv",
        [((A_ROWS, D), BF), ((E_ROWS, D), F32), ((B_ROWS, D), F32), ((ROWS, D), F32)],
        tile_rel, emb_rows, rel_weight, src_rows, band_dst, bound, part, to_up, to_down, from_low,
        from_high,
    )
    gw, local = call(
        relation_kernel,
        "ssssvvvvvvvvvv",
        [((Z, RELS, D), BF), ((ROWS, D), F32)],
        tile_rel, band_rel, live_tiles, neg_tiles, far, q, rows, band_rows, dq_band, rel_weight,
        src_rows, band_src, dst_rows, back,
    )
    gw = lax.all_to_all(gw, "z", split_axis=0, concat_axis=0, tiled=True)
    keep, give, _ = call(
        partner_kernel,
        "svvvvv",
        [((HALF, D), F32), ((HALF, D), BF), ((ROWS, D), F32)],
        core, far, got, emb_rows, rel_weight, local,
    )
    half = (keep + trade(give, 1).astype(F32)).astype(BF)
    mine = (half.astype(F32) + trade(half, 2).astype(F32)).astype(BF)
    other = trade(mine, 1)
    new_t, fresh = call(
        final_kernel,
        "svvvv",
        [((D, ROWS), F32), ((1, ROWS), F32)],
        core, mine, other, emb.T, emb_state.reshape(1, ROWS),
    )
    gw = jnp.sum(gw.astype(F32), axis=0).astype(BF)
    gw = lax.all_to_all(
        jnp.broadcast_to(gw[None], (XY, RELS, D)), ("x", "yh"), split_axis=0, concat_axis=0, tiled=True
    )
    gw = jnp.sum(gw.astype(F32), axis=0)
    rel_new = rel_weight - step_rate * gw / jnp.sqrt(rel_state + jnp.mean(gw * gw, axis=1))[:, None]
    return (new_t.T, fresh.reshape(ROWS), rel_new)


def solution(mesh):
    fine = Mesh(mesh.devices.reshape(4, 2, Z, N_REL), ("x", "yh", "z", "rel"))
    in_specs = (
        P(DOM, None),
        P(DOM),
        P("rel", None),
        P("rel"),
        P(),
        P("rel", DOM),
        P("rel", DOM),
        P("rel", DOM),
        P("rel", DOM),
        P("rel", DOM),
        P(DOM),
        P("rel", DOM),
        P("rel", DOM),
        P("rel", DOM),
    )
    out_specs = (P(DOM, None), P(DOM), P("rel", None))
    return jax.shard_map(body, mesh=fine, in_specs=in_specs, out_specs=out_specs, check_vma=False)
```

```python
import jax
import jax.numpy as jnp
from jax import lax
from jax.experimental import pallas as pl
from jax.experimental.pallas import tpu as pltpu
from jax.sharding import Mesh
from jax.sharding import PartitionSpec as P

step_rate = 0.25

D = 400
TILE = 128
ROWS = 256
BND = 128
E_ROWS = 512
B_ROWS = 256
A_ROWS = E_ROWS + B_ROWS
E_TILES = E_ROWS // TILE
B_TILES = B_ROWS // TILE
A_TILES = E_TILES + B_TILES
N_REL = 4
INFO = 8
SENT = ROWS + INFO
RELS = 8
NEG_TILES = 8
NEG = NEG_TILES * TILE
RIM = BND + B_ROWS + INFO

BF = jnp.bfloat16
F32 = jnp.float32
DOM = ("x", "yh", "z")
Z = 16
XY = 8


def vmem():
    return pl.BlockSpec(memory_space=pltpu.VMEM)


def smem():
    return pl.BlockSpec(memory_space=pltpu.SMEM)


def call(kernel, ins, outs, *args):
    return pl.pallas_call(
        kernel,
        in_specs=[smem() if kind == "s" else vmem() for kind in ins],
        out_specs=[vmem() for _ in outs],
        out_shape=[jax.ShapeDtypeStruct(shape, dtype) for shape, dtype in outs],
    )(*args)


def mm(a, b, dims):
    return lax.dot_general(a, b, (dims, ((), ())), preferred_element_type=F32)


NN = ((1,), (0,))
NT = ((1,), (1,))
TN = ((0,), (0,))


def two(values):
    high = values.astype(BF)
    return high, (values - high.astype(F32)).astype(BF)


def mm_two(a, b, dims):
    high, low = two(a)
    return mm(high, b, dims) + mm(low, b, dims)


def hits(rows, ids):
    return lax.broadcasted_iota(jnp.int32, (rows, ids.shape[1]), 0) == ids


def picks(rows, ids):
    return hits(rows, ids).astype(F32).astype(BF)


def row_of(lists):
    row = lax.broadcasted_iota(jnp.int32, (INFO, D), 0)
    block = jnp.zeros((INFO, D), F32)
    for k, values in enumerate(lists):
        if values.shape[1] < D:
            values = jnp.concatenate([values, jnp.zeros((1, D - values.shape[1]), F32)], axis=1)
        block = jnp.where(row == k, values, block)
    return block.astype(BF)


def start_kernel(
    tile_ref, band_ref, live_ref, neg_ref, embt_ref, relw_ref, src_ref, dst_ref, bsrc_ref,
    bdst_ref, bound_ref,
    emb_ref, part_ref, up_ref, down_ref, brows_ref,
):
    emb = embt_ref[...].T
    emb_ref[...] = emb
    emb_high, emb_low = two(emb)
    part_ref[:ROWS, :] = emb_high
    lane = lax.broadcasted_iota(jnp.int32, (1, D), 1)
    second = neg_ref[0, 0]
    for t in range(1, NEG_TILES):
        second = second + neg_ref[0, t]
    numbers = [tile_ref[0, t] for t in range(E_TILES)] + [band_ref[0, t] for t in range(B_TILES)]
    numbers += [live_ref[0, 0], second]
    scalars = jnp.zeros((1, D), F32)
    for k, number in enumerate(numbers):
        scalars = jnp.where(lane == k, number.astype(F32), scalars)
    part_ref[ROWS:, :] = row_of(
        [
            src_ref[:, :256].astype(F32),
            src_ref[:, 256:].astype(F32),
            dst_ref[:, :256].astype(F32),
            dst_ref[:, 256:].astype(F32),
            bsrc_ref[...].astype(F32),
            scalars,
        ]
    )
    rim = mm(picks(ROWS, bound_ref[...]), emb_high, TN).astype(BF)
    up_ref[:BND, :] = rim[BND:]
    down_ref[:BND, :] = rim[:BND]
    pick = picks(ROWS, bsrc_ref[...])
    rows = mm(pick, emb_high, TN) + mm(pick, emb_low, TN)
    brows_ref[...] = rows
    for t in range(B_TILES):
        q = (rows[t * TILE : (t + 1) * TILE] * relw_ref[pl.ds(band_ref[0, t], 1), :]).astype(BF)
        up_ref[BND + t * TILE : BND + (t + 1) * TILE, :] = q
        down_ref[BND + t * TILE : BND + (t + 1) * TILE, :] = q
    info = row_of([bdst_ref[...].astype(F32)])
    up_ref[BND + B_ROWS :, :] = info
    down_ref[BND + B_ROWS :, :] = info


def source_kernel(
    tile_ref, emb_ref, relw_ref, src_ref, bdst_ref, bound_ref, own_up_ref, own_down_ref,
    low_ref, high_ref,
    q_ref, rows_ref, dqb_ref, back_ref,
):
    emb_high, emb_low = two(emb_ref[...])
    pick = picks(ROWS, src_ref[...])
    rows = mm(pick, emb_high, TN) + mm(pick, emb_low, TN)
    rows_ref[...] = rows
    for t in range(E_TILES):
        at = slice(t * TILE, (t + 1) * TILE)
        q_ref[at, :] = (rows[at] * relw_ref[pl.ds(tile_ref[0, t], 1), :]).astype(BF)
    qb = own_up_ref[BND : BND + B_ROWS, :]
    q_ref[E_ROWS:, :] = qb
    near = jnp.concatenate([low_ref[:BND, :], high_ref[:BND, :]], axis=0)
    hit = hits(2 * BND, bdst_ref[...])
    pos = jnp.sum(jnp.where(hit, mm(near, qb, NT), 0.0), axis=0, keepdims=True)
    dqb_ref[...] = mm_two(jnp.where(hit, -jax.nn.sigmoid(-pos), 0.0), near, TN)
    grads = []
    for got_ref, mine_ref, shift in ((low_ref, own_down_ref, BND), (high_ref, own_up_ref, 0)):
        qn = got_ref[BND : BND + B_ROWS, :]
        ids = got_ref[BND + B_ROWS :, :].astype(F32)[:1, :B_ROWS].astype(jnp.int32) - shift
        hit = hits(BND, ids)
        pos = jnp.sum(jnp.where(hit, mm(mine_ref[:BND, :], qn, NT), 0.0), axis=0, keepdims=True)
        grads.append(mm_two(jnp.where(hit, -jax.nn.sigmoid(-pos), 0.0), qn, NN))
    high, low = two(jnp.concatenate(grads, axis=0))
    pick = picks(ROWS, bound_ref[...])
    back_ref[...] = mm(pick, high, NN) + mm(pick, low, NN)


def coefficients(scores, dst, live, second):
    edge = lax.broadcasted_iota(jnp.int32, (1, A_ROWS), 1)
    valid = jnp.where((edge < live * TILE) | (edge >= E_ROWS), 1.0, 0.0)
    hit = hits(ROWS, dst)
    pos = jnp.sum(jnp.where(hit, scores[:, :E_ROWS], 0.0), axis=0, keepdims=True)
    dpos = -jax.nn.sigmoid(-pos) * valid[:, :E_ROWS]
    counts = jnp.where(
        lax.broadcasted_iota(jnp.int32, (ROWS, 1), 0) < TILE, NEG_TILES - second, second
    )
    dneg = (jax.nn.sigmoid(scores) * (valid / NEG)).astype(BF).astype(F32) * counts
    return jnp.concatenate(
        [dneg[:, :E_ROWS] + jnp.where(hit, dpos, 0.0), dneg[:, E_ROWS:]], axis=1
    )


def relation_kernel(
    tile_ref, band_ref, live_ref, neg_ref, got_ref, q_ref, rows_ref, brows_ref, dqb_ref, relw_ref,
    dst_ref,
    gw_ref, step_ref,
):
    far = got_ref[:ROWS, :]
    second = neg_ref[0, 0]
    for t in range(1, NEG_TILES):
        second = second + neg_ref[0, t]
    scores = mm(far, q_ref[...], NT)
    coef = coefficients(scores, dst_ref[...], live_ref[0, 0], second.astype(F32))
    dq = mm_two(coef, far, TN)
    gw = jnp.zeros((RELS, D), F32)
    row8 = lax.broadcasted_iota(jnp.int32, (RELS, 1), 0)
    for t in range(A_TILES):
        piece = dq[t * TILE : (t + 1) * TILE]
        if t < E_TILES:
            ident = tile_ref[0, t]
            rows = rows_ref[t * TILE : (t + 1) * TILE, :]
        else:
            at = slice((t - E_TILES) * TILE, (t - E_TILES + 1) * TILE)
            ident = band_ref[0, t - E_TILES]
            rows = brows_ref[at, :]
            piece = piece + dqb_ref[at, :]
        gw = gw + jnp.where(row8 == ident, jnp.sum(piece * rows, axis=0, keepdims=True), 0.0)
        step_ref[t * TILE : (t + 1) * TILE, :] = piece * relw_ref[pl.ds(ident, 1), :]
    for k in range(Z):
        gw_ref[k, :, :] = gw.astype(BF)


def partner_kernel(
    got_ref, part_ref, relw_ref, step_ref, src_ref, bsrc_ref, back_ref,
    total_ref,
):
    far = got_ref[:ROWS, :]
    info = got_ref[ROWS:, :].astype(F32)
    src = jnp.concatenate([info[0:1, :256], info[1:2, :256], info[4:5, :256]], axis=1)
    dst = jnp.concatenate([info[2:3, :256], info[3:4, :256]], axis=1).astype(jnp.int32)
    rows = mm(picks(ROWS, src.astype(jnp.int32)), far, TN)
    row8 = lax.broadcasted_iota(jnp.int32, (RELS, 1), 0)
    parts = []
    for t in range(A_TILES):
        chosen = row8 == info[5:6, t : t + 1].astype(jnp.int32)
        w = jnp.sum(jnp.where(chosen, relw_ref[...], 0.0), axis=0, keepdims=True)
        parts.append((rows[t * TILE : (t + 1) * TILE] * w).astype(BF))
    q = jnp.concatenate(parts, axis=0)
    scores = mm(part_ref[:ROWS, :], q, NT)
    coef = coefficients(
        scores, dst, info[5:6, A_TILES : A_TILES + 1].astype(jnp.int32), info[5:6, A_TILES + 1 : A_TILES + 2]
    )
    high, low = two(step_ref[...])
    pick = jnp.concatenate([picks(ROWS, src_ref[...]), picks(ROWS, bsrc_ref[...])], axis=1)
    total_ref[...] = (
        back_ref[...] + mm(pick, high, NN) + mm(pick, low, NN) + mm_two(coef, q, NN)
    )


def final_kernel(mine_ref, other_ref, embt_ref, state_ref, new_ref, fresh_ref):
    grad = (mine_ref[...].astype(F32) + other_ref[...].astype(F32)).T
    fresh = state_ref[...] + jnp.sum(grad * grad, axis=0, keepdims=True) / D
    fresh_ref[...] = fresh
    new_ref[...] = embt_ref[...] - step_rate * grad / jnp.sqrt(fresh)


def swap(axes, size, number, block, work):
    def branch(k):
        def run(moved, *args):
            if k:
                moved = lax.ppermute(moved, axes, [(i, i ^ k) for i in range(size)])
            return (moved, *work(*args))

        return run

    return lambda *args: lax.switch(number, [branch(k) for k in range(size)], block, *args)


def trade(values, bit):
    return lax.ppermute(values, "rel", [(i, i ^ bit) for i in range(N_REL)])


def body(
    emb, emb_state, rel_weight, rel_state, swap_mask, src_rows, dst_rows, tile_rel, live_tiles,
    neg_tiles, bound_rows, band_src, band_dst, band_rel,
):
    mask = swap_mask[0]
    bound = bound_rows.reshape(1, 2 * BND)
    count = lax.axis_size(DOM)
    part_shape, rim_shape = (SENT, D), (RIM, D)
    emb_rows, part, to_up, to_down, band_rows = call(
        start_kernel,
        "ssssvvvvvvv",
        [((ROWS, D), F32), (part_shape, BF), (rim_shape, BF), (rim_shape, BF), ((B_ROWS, D), F32)],
        tile_rel, band_rel, live_tiles, neg_tiles, emb.T, rel_weight, src_rows, dst_rows, band_src,
        band_dst, bound,
    )
    from_low = lax.ppermute(to_up, DOM, [(i, i + 1) for i in range(count - 1)])
    from_high = lax.ppermute(to_down, DOM, [(i + 1, i) for i in range(count - 1)])
    (got,) = swap(("x", "yh"), XY, lax.shift_right_logical(mask, 4), part, lambda: ())()

    def sources(*args):
        return call(
            source_kernel,
            "svvvvvvvvv",
            [((A_ROWS, D), BF), ((E_ROWS, D), F32), ((B_ROWS, D), F32), ((ROWS, D), F32)],
            *args,
        )

    got, q, rows, dq_band, back = swap("z", Z, lax.bitwise_and(mask, 15), got, sources)(
        tile_rel, emb_rows, rel_weight, src_rows, band_dst, bound, to_up, to_down, from_low, from_high
    )
    gw, step = call(
        relation_kernel,
        "ssssvvvvvvv",
        [((Z, RELS, D), BF), ((A_ROWS, D), F32)],
        tile_rel, band_rel, live_tiles, neg_tiles, got, q, rows, band_rows, dq_band, rel_weight,
        dst_rows,
    )
    gw = lax.all_to_all(gw, "z", split_axis=0, concat_axis=0, tiled=True)
    (total,) = call(
        partner_kernel,
        "vvvvvvv",
        [((ROWS, D), F32)],
        got, part, rel_weight, step, src_rows, band_src, back,
    )
    pair = (total + trade(total, 1)).astype(BF)
    other = trade(pair, 2)
    new_t, fresh = call(
        final_kernel,
        "vvvv",
        [((D, ROWS), F32), ((1, ROWS), F32)],
        pair, other, emb.T, emb_state.reshape(1, ROWS),
    )
    gw = jnp.sum(gw.astype(F32), axis=0).astype(BF)
    gw = jnp.broadcast_to(gw[None], (XY, RELS, D))
    gw = lax.all_to_all(gw, ("x", "yh"), split_axis=0, concat_axis=0, tiled=True)
    gw = jnp.sum(gw.astype(F32), axis=0)
    rel_new = rel_weight - step_rate * gw / jnp.sqrt(rel_state + jnp.mean(gw * gw, axis=1))[:, None]
    return (new_t.T, fresh.reshape(ROWS), rel_new)


def solution(mesh):
    fine = Mesh(mesh.devices.reshape(4, 2, Z, N_REL), ("x", "yh", "z", "rel"))
    in_specs = (
        P(DOM, None),
        P(DOM),
        P("rel", None),
        P("rel"),
        P(),
        P("rel", DOM),
        P("rel", DOM),
        P("rel", DOM),
        P("rel", DOM),
        P("rel", DOM),
        P(DOM),
        P("rel", DOM),
        P("rel", DOM),
        P("rel", DOM),
    )
    out_specs = (P(DOM, None), P(DOM), P("rel", None))
    return jax.shard_map(
        body, mesh=fine, in_specs=in_specs, out_specs=out_specs, check_vma=False
    )
```

```python
import jax
import jax.numpy as jnp
from jax import lax
from jax.experimental import pallas as pl
from jax.experimental.pallas import tpu as pltpu
from jax.sharding import Mesh
from jax.sharding import PartitionSpec as P

step_rate = 0.25

D = 400
TILE = 128
ROWS = 256
HALF = ROWS // 2
BND = 128
E_ROWS = 512
B_ROWS = 256
A_ROWS = E_ROWS + B_ROWS
E_TILES = E_ROWS // TILE
B_TILES = B_ROWS // TILE
A_TILES = E_TILES + B_TILES
N_REL = 4
RELS = 8
NEG_TILES = 8
NEG = NEG_TILES * TILE
INFO = 16
SENT = D + INFO
RIM_INFO = 8
RIM = D + RIM_INFO
RIM_WIDTH = BND + B_ROWS

BF = jnp.bfloat16
F32 = jnp.float32
DOM = ("x", "yh", "z")
Z = 16
XY = 8


def vmem():
    return pl.BlockSpec(memory_space=pltpu.VMEM)


def smem():
    return pl.BlockSpec(memory_space=pltpu.SMEM)


def call(kernel, ins, outs, *args):
    return pl.pallas_call(
        kernel,
        in_specs=[smem() if kind == "s" else vmem() for kind in ins],
        out_specs=[vmem() for _ in outs],
        out_shape=[jax.ShapeDtypeStruct(shape, dtype) for shape, dtype in outs],
    )(*args)


def mm(a, b, dims):
    return lax.dot_general(a, b, (dims, ((), ())), preferred_element_type=F32)


NN = ((1,), (0,))
NT = ((1,), (1,))
TN = ((0,), (0,))


def two(values):
    high = values.astype(BF)
    return high, (values - high.astype(F32)).astype(BF)


def mm_two(a, b, dims):
    high, low = two(a)
    return mm(high, b, dims) + mm(low, b, dims)


def hits(count, ids):
    return lax.broadcasted_iota(jnp.int32, (count, ids.shape[1]), 0) == ids


def ones(mask):
    return mask.astype(F32).astype(BF)


def stacked(count, width, lists):
    row = lax.broadcasted_iota(jnp.int32, (count, width), 0)
    block = jnp.zeros((count, width), F32)
    for k, values in enumerate(lists):
        values = values.astype(F32)
        if values.shape[1] < width:
            values = jnp.concatenate(
                [values, jnp.zeros((1, width - values.shape[1]), F32)], axis=1
            )
        block = jnp.where(row == k, values, block)
    return block.astype(BF)


def relations(ids):
    spread = [jnp.broadcast_to(ident, (1, TILE)).astype(jnp.int32) for ident in ids]
    return ones(hits(RELS, jnp.concatenate(spread, axis=1)))


def weights(relw, chosen):
    high = relw.astype(BF)
    rest = relw - high.astype(F32)
    middle = rest.astype(BF)
    low = (rest - middle.astype(F32)).astype(BF)
    return (mm(high, chosen, TN) + mm(middle, chosen, TN)) + mm(low, chosen, TN)


def tile_ids(tile_ref, band_ref):
    return [tile_ref[0, t] for t in range(E_TILES)], [band_ref[0, t] for t in range(B_TILES)]


def second_count(neg_ref):
    second = neg_ref[0, 0]
    for t in range(1, NEG_TILES):
        second = second + neg_ref[0, t]
    return second


def start_kernel(
    core_ref, tile_ref, band_ref, live_ref, neg_ref, emb_ref, relw_ref, src_ref, dst_ref, bsrc_ref,
    bdst_ref, bound_ref,
    part_ref, up_ref, down_ref, brows_ref,
):
    high, low = two(emb_ref[...])
    part_ref[:D, :] = jnp.where(core_ref[0] == 0, high[:, :HALF], high[:, HALF:])
    edge_ids, band_ids = tile_ids(tile_ref, band_ref)
    lane = lax.broadcasted_iota(jnp.int32, (1, TILE), 1)
    scalars = jnp.zeros((1, TILE), F32)
    for k, number in enumerate([*edge_ids, *band_ids, live_ref[0, 0], second_count(neg_ref)]):
        scalars = jnp.where(lane == k, number.astype(F32), scalars)
    lists = []
    for ref in (src_ref, bsrc_ref, dst_ref):
        lists += [ref[:, k : k + TILE] for k in range(0, ref.shape[1], TILE)]
    part_ref[D:, :] = stacked(INFO, TILE, [*lists, scalars])
    rim = mm(high, ones(hits(ROWS, bound_ref[...])), NN).astype(BF)
    up_ref[:D, :BND] = rim[:, BND:]
    down_ref[:D, :BND] = rim[:, :BND]
    pick = ones(hits(ROWS, bsrc_ref[...]))
    rows = mm(high, pick, NN) + mm(low, pick, NN)
    brows_ref[...] = rows
    q = (rows * weights(relw_ref[...], relations(band_ids))).astype(BF)
    info = stacked(RIM_INFO, RIM_WIDTH, [bdst_ref[...]])
    for ref in (up_ref, down_ref):
        ref[:D, BND:] = q
        ref[D:, :] = info


def pull(scores, hit):
    pos = jnp.sum(jnp.where(hit, scores, 0.0), axis=0, keepdims=True)
    return jnp.where(hit, -jax.nn.sigmoid(-pos), 0.0)


def source_kernel(
    tile_ref, band_ref, emb_ref, relw_ref, src_ref, bdst_ref, bound_ref, own_up_ref, own_down_ref,
    low_ref, high_ref,
    q_ref, rows_ref, dqb_ref, back_ref,
):
    high, low = two(emb_ref[...])
    pick = ones(hits(ROWS, src_ref[...]))
    rows = mm(high, pick, NN) + mm(low, pick, NN)
    rows_ref[...] = rows
    edge_ids, _ = tile_ids(tile_ref, band_ref)
    q_ref[:, :E_ROWS] = (rows * weights(relw_ref[...], relations(edge_ids))).astype(BF)
    qb = own_up_ref[:D, BND:]
    q_ref[:, E_ROWS:] = qb
    near = jnp.concatenate([low_ref[:D, :BND], high_ref[:D, :BND]], axis=1)
    first, second = two(pull(mm(near, qb, TN), hits(2 * BND, bdst_ref[...])))
    dqb_ref[...] = mm(near, first, NN) + mm(near, second, NN)
    grads = []
    for got_ref, mine_ref, shift in ((low_ref, own_down_ref, BND), (high_ref, own_up_ref, 0)):
        qn = got_ref[:D, BND:]
        ids = got_ref[D:, :].astype(F32)[:1, :B_ROWS].astype(jnp.int32) - shift
        first, second = two(pull(mm(mine_ref[:D, :BND], qn, TN), hits(BND, ids)))
        grads.append(mm(qn, first, NT) + mm(qn, second, NT))
    back_ref[...] = mm_two(jnp.concatenate(grads, axis=1), ones(hits(ROWS, bound_ref[...])), NT)


def coefficients(scores, dst, live, second):
    edge = lax.broadcasted_iota(jnp.int32, (1, A_ROWS), 1)
    valid = jnp.where((edge < live * TILE) | (edge >= E_ROWS), 1.0, 0.0)
    counts = jnp.where(
        lax.broadcasted_iota(jnp.int32, (ROWS, 1), 0) < TILE, NEG_TILES - second, second
    )
    dneg = (jax.nn.sigmoid(scores) * (valid / NEG)).astype(BF).astype(F32) * counts
    positive = pull(scores[:, :E_ROWS], hits(ROWS, dst)) * valid[:, :E_ROWS]
    return two(jnp.concatenate([dneg[:, :E_ROWS] + positive, dneg[:, E_ROWS:]], axis=1))


def far_block(core_ref, got_ref, other_ref):
    got, other = got_ref[:D, :], other_ref[:D, :]
    first = core_ref[0] == 0
    return jnp.concatenate([jnp.where(first, got, other), jnp.where(first, other, got)], axis=1)


def relation_kernel(
    core_ref, tile_ref, band_ref, live_ref, neg_ref, got_ref, other_ref, q_ref, rows_ref, brows_ref,
    dqb_ref, relw_ref, dst_ref,
    gw_ref, step_ref,
):
    far = far_block(core_ref, got_ref, other_ref)
    scores = mm(far, q_ref[...], TN)
    high, low = coefficients(
        scores, dst_ref[...], live_ref[0, 0], second_count(neg_ref).astype(F32)
    )
    edge_ids, band_ids = tile_ids(tile_ref, band_ref)
    chosen = relations(edge_ids + band_ids)
    dq = mm(far, high, NN) + mm(far, low, NN)
    dq_band = dq[:, E_ROWS:] + dqb_ref[...]
    first, second = two(dq[:, :E_ROWS] * rows_ref[...])
    third, fourth = two(dq_band * brows_ref[...])
    gw = (mm(chosen[:, :E_ROWS], first, NT) + mm(chosen[:, :E_ROWS], second, NT)) + (
        mm(chosen[:, E_ROWS:], third, NT) + mm(chosen[:, E_ROWS:], fourth, NT)
    )
    gw = gw.astype(BF)
    for k in range(Z):
        gw_ref[k, :, :] = gw
    step_ref[:, :E_ROWS] = dq[:, :E_ROWS]
    step_ref[:, E_ROWS:] = dq_band


def partner_kernel(
    core_ref, tile_ref, band_ref, got_ref, other_ref, emb_ref, relw_ref, step_ref, src_ref, bsrc_ref,
    back_ref,
    total_ref,
):
    far = far_block(core_ref, got_ref, other_ref)
    info = got_ref[D:, :].astype(F32)
    ids = jnp.concatenate([info[k : k + 1, :] for k in range(10)], axis=1).astype(jnp.int32)
    scalars = info[10:11, :]
    relw = relw_ref[...]
    chosen = relations([scalars[:, t : t + 1] for t in range(A_TILES)])
    q = (mm(far, ones(hits(ROWS, ids[:, :A_ROWS])), NN) * weights(relw, chosen)).astype(BF)
    scores = mm(emb_ref[...].astype(BF), q, TN)
    high, low = coefficients(
        scores,
        ids[:, A_ROWS:],
        scalars[:, A_TILES : A_TILES + 1].astype(jnp.int32),
        scalars[:, A_TILES + 1 : A_TILES + 2],
    )
    edge_ids, band_ids = tile_ids(tile_ref, band_ref)
    steps = step_ref[...] * weights(relw, relations(edge_ids + band_ids))
    pick = jnp.concatenate([ones(hits(ROWS, src_ref[...])), ones(hits(ROWS, bsrc_ref[...]))], axis=1)
    total_ref[...] = (
        back_ref[...] + mm_two(steps, pick, NT) + mm(q, high, NT) + mm(q, low, NT)
    )


def final_kernel(mine_ref, other_ref, emb_ref, state_ref, new_ref, fresh_ref):
    grad = mine_ref[...].astype(F32) + other_ref[...].astype(F32)
    fresh = state_ref[...] + jnp.sum(grad * grad, axis=0, keepdims=True) / D
    fresh_ref[...] = fresh
    new_ref[...] = emb_ref[...] - step_rate * grad / jnp.sqrt(fresh)


def swap(axes, size, number, work):
    def branch(k):
        def run(moved, *args):
            if k:
                moved = lax.ppermute(moved, axes, [(i, i ^ k) for i in range(size)])
            return (moved, *work(*args))

        return run

    return lambda *args: lax.switch(number, [branch(k) for k in range(size)], *args)


def trade(values, bit):
    return lax.ppermute(values, "rel", [(i, i ^ bit) for i in range(N_REL)])


def body(
    emb, emb_state, rel_weight, rel_state, swap_mask, src_rows, dst_rows, tile_rel, live_tiles,
    neg_tiles, bound_rows, band_src, band_dst, band_rel,
):
    mask = swap_mask[0]
    bound = bound_rows.reshape(1, 2 * BND)
    core = lax.bitwise_and(lax.axis_index("rel").astype(jnp.int32), 1).reshape(1)
    count = lax.axis_size(DOM)
    emb_t = emb.T
    part, to_up, to_down, band_rows = call(
        start_kernel,
        "sssssvvvvvvv",
        [((SENT, HALF), BF), ((RIM, RIM_WIDTH), BF), ((RIM, RIM_WIDTH), BF), ((D, B_ROWS), F32)],
        core, tile_rel, band_rel, live_tiles, neg_tiles, emb_t, rel_weight, src_rows, dst_rows,
        band_src, band_dst, bound,
    )
    from_low = lax.ppermute(to_up, DOM, [(i, i + 1) for i in range(count - 1)])
    from_high = lax.ppermute(to_down, DOM, [(i + 1, i) for i in range(count - 1)])
    (got,) = swap(("x", "yh"), XY, lax.shift_right_logical(mask, 4), lambda: ())(part)

    def sources(*args):
        return call(
            source_kernel,
            "ssvvvvvvvvv",
            [((D, A_ROWS), BF), ((D, E_ROWS), F32), ((D, B_ROWS), F32), ((D, ROWS), F32)],
            *args,
        )

    got, q, rows, dq_band, back = swap("z", Z, lax.bitwise_and(mask, 15), sources)(
        got, tile_rel, band_rel, emb_t, rel_weight, src_rows, band_dst, bound, to_up, to_down,
        from_low, from_high,
    )
    other_half = trade(got, 1)
    gw, step = call(
        relation_kernel,
        "sssssvvvvvvvv",
        [((Z, RELS, D), BF), ((D, A_ROWS), F32)],
        core, tile_rel, band_rel, live_tiles, neg_tiles, got, other_half, q, rows, band_rows,
        dq_band, rel_weight, dst_rows,
    )
    gw = lax.all_to_all(gw, "z", split_axis=0, concat_axis=0, tiled=True)
    (total,) = call(
        partner_kernel,
        "sssvvvvvvvv",
        [((D, ROWS), F32)],
        core, tile_rel, band_rel, got, other_half, emb_t, rel_weight, step, src_rows,
        band_src, back,
    )
    pair = (total + trade(total, 1)).astype(BF)
    other = trade(pair, 2)
    new_t, fresh = call(
        final_kernel,
        "vvvv",
        [((D, ROWS), F32), ((1, ROWS), F32)],
        pair, other, emb_t, emb_state.reshape(1, ROWS),
    )
    gw = jnp.sum(gw.astype(F32), axis=0).astype(BF)
    gw = jnp.broadcast_to(gw[None], (XY, RELS, D))
    gw = lax.all_to_all(gw, ("x", "yh"), split_axis=0, concat_axis=0, tiled=True)
    gw = jnp.sum(gw.astype(F32), axis=0)
    rel_new = rel_weight - step_rate * gw / jnp.sqrt(rel_state + jnp.mean(gw * gw, axis=1))[:, None]
    return (new_t.T, fresh.reshape(ROWS), rel_new)


def solution(mesh):
    fine = Mesh(mesh.devices.reshape(4, 2, Z, N_REL), ("x", "yh", "z", "rel"))
    in_specs = (
        P(DOM, None),
        P(DOM),
        P("rel", None),
        P("rel"),
        P(),
        P("rel", DOM),
        P("rel", DOM),
        P("rel", DOM),
        P("rel", DOM),
        P("rel", DOM),
        P(DOM),
        P("rel", DOM),
        P("rel", DOM),
        P("rel", DOM),
    )
    out_specs = (P(DOM, None), P(DOM), P("rel", None))
    return jax.shard_map(
        body, mesh=fine, in_specs=in_specs, out_specs=out_specs, check_vma=False
    )
```

```python
import jax
import jax.numpy as jnp
from jax import lax
from jax.experimental import pallas as pl
from jax.experimental.pallas import tpu as pltpu
from jax.sharding import Mesh
from jax.sharding import PartitionSpec as P

step_rate = 0.25

D = 400
TILE = 128
ROWS = 256
HALF = ROWS // 2
BND = 128
E_ROWS = 512
B_ROWS = 256
A_ROWS = E_ROWS + B_ROWS
E_TILES = E_ROWS // TILE
B_TILES = B_ROWS // TILE
A_TILES = E_TILES + B_TILES
N_REL = 4
RELS = 8
NEG_TILES = 8
NEG = NEG_TILES * TILE
INFO = 16
SENT = D + INFO
RIM_INFO = 8
RIM = D + RIM_INFO
RIM_WIDTH = BND + B_ROWS

BF = jnp.bfloat16
F32 = jnp.float32
DOM = ("x", "yh", "z")
Z = 16
XY = 8


def vmem():
    return pl.BlockSpec(memory_space=pltpu.VMEM)


def smem():
    return pl.BlockSpec(memory_space=pltpu.SMEM)


def call(kernel, ins, outs, *args):
    return pl.pallas_call(
        kernel,
        in_specs=[smem() if kind == "s" else vmem() for kind in ins],
        out_specs=[vmem() for _ in outs],
        out_shape=[jax.ShapeDtypeStruct(shape, dtype) for shape, dtype in outs],
    )(*args)


def mm(a, b, dims):
    return lax.dot_general(a, b, (dims, ((), ())), preferred_element_type=F32)


NN = ((1,), (0,))
NT = ((1,), (1,))
TN = ((0,), (0,))


def two(values):
    high = values.astype(BF)
    return high, (values - high.astype(F32)).astype(BF)


def mm_two(a, b, dims):
    high, low = two(a)
    return mm(high, b, dims) + mm(low, b, dims)


def hits(count, ids):
    return lax.broadcasted_iota(jnp.int32, (count, ids.shape[1]), 0) == ids


def ones(mask):
    return mask.astype(F32).astype(BF)


def stacked(count, width, lists):
    row = lax.broadcasted_iota(jnp.int32, (count, width), 0)
    block = jnp.zeros((count, width), F32)
    for k, values in enumerate(lists):
        values = values.astype(F32)
        if values.shape[1] < width:
            values = jnp.concatenate(
                [values, jnp.zeros((1, width - values.shape[1]), F32)], axis=1
            )
        block = jnp.where(row == k, values, block)
    return block.astype(BF)


def relations(ids):
    spread = [jnp.broadcast_to(ident, (1, TILE)).astype(jnp.int32) for ident in ids]
    return ones(hits(RELS, jnp.concatenate(spread, axis=1)))


def weights(relw, chosen):
    high = relw.astype(BF)
    rest = relw - high.astype(F32)
    middle = rest.astype(BF)
    low = (rest - middle.astype(F32)).astype(BF)
    return (mm(high, chosen, TN) + mm(middle, chosen, TN)) + mm(low, chosen, TN)


def tile_ids(tile_ref, band_ref):
    return [tile_ref[0, t] for t in range(E_TILES)], [band_ref[0, t] for t in range(B_TILES)]


def second_count(neg_ref):
    second = neg_ref[0, 0]
    for t in range(1, NEG_TILES):
        second = second + neg_ref[0, t]
    return second


def start_kernel(
    core_ref, tile_ref, band_ref, live_ref, neg_ref, emb_ref, relw_ref, src_ref, dst_ref, bsrc_ref,
    bdst_ref, bound_ref,
    part_ref, up_ref, down_ref, brows_ref,
):
    high, low = two(emb_ref[...])
    part_ref[:D, :] = jnp.where(core_ref[0] == 0, high[:, :HALF], high[:, HALF:])
    edge_ids, band_ids = tile_ids(tile_ref, band_ref)
    lane = lax.broadcasted_iota(jnp.int32, (1, TILE), 1)
    scalars = jnp.zeros((1, TILE), F32)
    for k, number in enumerate([*edge_ids, *band_ids, live_ref[0, 0], second_count(neg_ref)]):
        scalars = jnp.where(lane == k, number.astype(F32), scalars)
    lists = []
    for ref in (src_ref, bsrc_ref, dst_ref):
        lists += [ref[:, k : k + TILE] for k in range(0, ref.shape[1], TILE)]
    part_ref[D:, :] = stacked(INFO, TILE, [*lists, scalars])
    rim = mm(high, ones(hits(ROWS, bound_ref[...])), NN).astype(BF)
    up_ref[:D, :BND] = rim[:, BND:]
    down_ref[:D, :BND] = rim[:, :BND]
    pick = ones(hits(ROWS, bsrc_ref[...]))
    rows = mm(high, pick, NN) + mm(low, pick, NN)
    brows_ref[...] = rows
    q = (rows * weights(relw_ref[...], relations(band_ids))).astype(BF)
    info = stacked(RIM_INFO, RIM_WIDTH, [bdst_ref[...]])
    for ref in (up_ref, down_ref):
        ref[:D, BND:] = q
        ref[D:, :] = info


def pull(scores, hit):
    pos = jnp.sum(jnp.where(hit, scores, 0.0), axis=0, keepdims=True)
    return jnp.where(hit, -jax.nn.sigmoid(-pos), 0.0)


def source_kernel(
    tile_ref, band_ref, emb_ref, relw_ref, src_ref, bdst_ref, bound_ref, own_up_ref, own_down_ref,
    low_ref, high_ref,
    q_ref, rows_ref, dqb_ref, back_ref,
):
    high, low = two(emb_ref[...])
    pick = ones(hits(ROWS, src_ref[...]))
    rows = mm(high, pick, NN) + mm(low, pick, NN)
    rows_ref[...] = rows
    edge_ids, _ = tile_ids(tile_ref, band_ref)
    q_ref[:, :E_ROWS] = (rows * weights(relw_ref[...], relations(edge_ids))).astype(BF)
    qb = own_up_ref[:D, BND:]
    q_ref[:, E_ROWS:] = qb
    near = jnp.concatenate([low_ref[:D, :BND], high_ref[:D, :BND]], axis=1)
    first, second = two(pull(mm(near, qb, TN), hits(2 * BND, bdst_ref[...])))
    dqb_ref[...] = mm(near, first, NN) + mm(near, second, NN)
    grads = []
    for got_ref, mine_ref, shift in ((low_ref, own_down_ref, BND), (high_ref, own_up_ref, 0)):
        qn = got_ref[:D, BND:]
        ids = got_ref[D:, :].astype(F32)[:1, :B_ROWS].astype(jnp.int32) - shift
        first, second = two(pull(mm(mine_ref[:D, :BND], qn, TN), hits(BND, ids)))
        grads.append(mm(qn, first, NT) + mm(qn, second, NT))
    back_ref[...] = mm_two(jnp.concatenate(grads, axis=1), ones(hits(ROWS, bound_ref[...])), NT)


def coefficients(scores, dst, live, second):
    edge = lax.broadcasted_iota(jnp.int32, (1, A_ROWS), 1)
    valid = jnp.where((edge < live * TILE) | (edge >= E_ROWS), 1.0, 0.0)
    counts = jnp.where(
        lax.broadcasted_iota(jnp.int32, (ROWS, 1), 0) < TILE, NEG_TILES - second, second
    )
    dneg = (jax.nn.sigmoid(scores) * (valid / NEG)).astype(BF).astype(F32) * counts
    positive = pull(scores[:, :E_ROWS], hits(ROWS, dst)) * valid[:, :E_ROWS]
    return two(jnp.concatenate([dneg[:, :E_ROWS] + positive, dneg[:, E_ROWS:]], axis=1))


def far_block(core_ref, got_ref, other_ref):
    got, other = got_ref[:D, :], other_ref[:D, :]
    first = core_ref[0] == 0
    return jnp.concatenate([jnp.where(first, got, other), jnp.where(first, other, got)], axis=1)


def relation_kernel(
    core_ref, tile_ref, band_ref, live_ref, neg_ref, got_ref, other_ref, q_ref, rows_ref, brows_ref,
    dqb_ref, relw_ref, dst_ref,
    gw_ref, step_ref,
):
    far = far_block(core_ref, got_ref, other_ref)
    scores = mm(far, q_ref[...], TN)
    high, low = coefficients(
        scores, dst_ref[...], live_ref[0, 0], second_count(neg_ref).astype(F32)
    )
    edge_ids, band_ids = tile_ids(tile_ref, band_ref)
    chosen = relations(edge_ids + band_ids)
    dq = mm(far, high, NN) + mm(far, low, NN)
    dq_band = dq[:, E_ROWS:] + dqb_ref[...]
    first, second = two(dq[:, :E_ROWS] * rows_ref[...])
    third, fourth = two(dq_band * brows_ref[...])
    gw = (mm(chosen[:, :E_ROWS], first, NT) + mm(chosen[:, :E_ROWS], second, NT)) + (
        mm(chosen[:, E_ROWS:], third, NT) + mm(chosen[:, E_ROWS:], fourth, NT)
    )
    gw = gw.astype(BF)
    for k in range(Z):
        gw_ref[k, :, :] = gw
    step_ref[:, :E_ROWS] = dq[:, :E_ROWS]
    step_ref[:, E_ROWS:] = dq_band


def partner_kernel(
    core_ref, tile_ref, band_ref, got_ref, other_ref, emb_ref, relw_ref, step_ref, src_ref, bsrc_ref,
    back_ref,
    total_ref,
):
    far = far_block(core_ref, got_ref, other_ref)
    info = got_ref[D:, :].astype(F32)
    ids = jnp.concatenate([info[k : k + 1, :] for k in range(10)], axis=1).astype(jnp.int32)
    scalars = info[10:11, :]
    relw = relw_ref[...]
    chosen = relations([scalars[:, t : t + 1] for t in range(A_TILES)])
    q = (mm(far, ones(hits(ROWS, ids[:, :A_ROWS])), NN) * weights(relw, chosen)).astype(BF)
    scores = mm(emb_ref[...].astype(BF), q, TN)
    high, low = coefficients(
        scores,
        ids[:, A_ROWS:],
        scalars[:, A_TILES : A_TILES + 1].astype(jnp.int32),
        scalars[:, A_TILES + 1 : A_TILES + 2],
    )
    edge_ids, band_ids = tile_ids(tile_ref, band_ref)
    steps = step_ref[...] * weights(relw, relations(edge_ids + band_ids))
    pick = jnp.concatenate([ones(hits(ROWS, src_ref[...])), ones(hits(ROWS, bsrc_ref[...]))], axis=1)
    total = back_ref[...] + mm_two(steps, pick, NT) + mm(q, high, NT) + mm(q, low, NT)
    total_ref[...] = total.astype(BF)


def final_kernel(own_ref, core_ref, far_ref, cross_ref, emb_ref, state_ref, new_ref, fresh_ref):
    near = own_ref[...].astype(F32) + core_ref[...].astype(F32)
    grad = near + (far_ref[...].astype(F32) + cross_ref[...].astype(F32))
    fresh = state_ref[...] + jnp.sum(grad * grad, axis=0, keepdims=True) / D
    fresh_ref[...] = fresh
    new_ref[...] = emb_ref[...] - step_rate * grad / jnp.sqrt(fresh)


def update_kernel(state_ref, gw_ref, relw_ref, new_ref):
    gw = gw_ref[0, :, :].astype(F32)
    for k in range(1, XY):
        gw = gw + gw_ref[k, :, :].astype(F32)
    row = lax.broadcasted_iota(jnp.int32, (RELS, 1), 0)
    state = jnp.zeros((RELS, 1), F32)
    for k in range(RELS):
        state = jnp.where(row == k, state_ref[k], state)
    fresh = state + jnp.sum(gw * gw, axis=1, keepdims=True) / D
    new_ref[...] = relw_ref[...] - step_rate * gw / jnp.sqrt(fresh)


def swap(axes, size, number, work):
    def branch(k):
        def run(moved, *args):
            if k:
                moved = lax.ppermute(moved, axes, [(i, i ^ k) for i in range(size)])
            return (moved, *work(*args))

        return run

    return lambda *args: lax.switch(number, [branch(k) for k in range(size)], *args)


def trade(values, bit):
    return lax.ppermute(values, "rel", [(i, i ^ bit) for i in range(N_REL)])


def body(
    emb, emb_state, rel_weight, rel_state, swap_mask, src_rows, dst_rows, tile_rel, live_tiles,
    neg_tiles, bound_rows, band_src, band_dst, band_rel,
):
    mask = swap_mask[0]
    bound = bound_rows.reshape(1, 2 * BND)
    core = lax.bitwise_and(lax.axis_index("rel").astype(jnp.int32), 1).reshape(1)
    count = lax.axis_size(DOM)
    emb_t = emb.T
    part, to_up, to_down, band_rows = call(
        start_kernel,
        "sssssvvvvvvv",
        [((SENT, HALF), BF), ((RIM, RIM_WIDTH), BF), ((RIM, RIM_WIDTH), BF), ((D, B_ROWS), F32)],
        core, tile_rel, band_rel, live_tiles, neg_tiles, emb_t, rel_weight, src_rows, dst_rows,
        band_src, band_dst, bound,
    )
    from_low = lax.ppermute(to_up, DOM, [(i, i + 1) for i in range(count - 1)])
    from_high = lax.ppermute(to_down, DOM, [(i + 1, i) for i in range(count - 1)])
    (got,) = swap("z", Z, lax.bitwise_and(mask, 15), lambda: ())(part)

    def sources(*args):
        return call(
            source_kernel,
            "ssvvvvvvvvv",
            [((D, A_ROWS), BF), ((D, E_ROWS), F32), ((D, B_ROWS), F32), ((D, ROWS), F32)],
            *args,
        )

    along_xy = swap(("x", "yh"), XY, lax.shift_right_logical(mask, 4), sources)
    got, q, rows, dq_band, back = along_xy(
        got, tile_rel, band_rel, emb_t, rel_weight, src_rows, band_dst, bound, to_up, to_down,
        from_low, from_high,
    )
    other_half = trade(got, 1)
    gw, step = call(
        relation_kernel,
        "sssssvvvvvvvv",
        [((Z, RELS, D), BF), ((D, A_ROWS), F32)],
        core, tile_rel, band_rel, live_tiles, neg_tiles, got, other_half, q, rows, band_rows,
        dq_band, rel_weight, dst_rows,
    )
    gw = lax.all_to_all(gw, "z", split_axis=0, concat_axis=0, tiled=True)
    (total,) = call(
        partner_kernel,
        "sssvvvvvvvv",
        [((D, ROWS), BF)],
        core, tile_rel, band_rel, got, other_half, emb_t, rel_weight, step, src_rows,
        band_src, back,
    )
    from_cross = trade(total, 3)
    from_y = trade(total, 2)
    from_core = trade(total, 1)
    new_t, fresh = call(
        final_kernel,
        "vvvvvv",
        [((D, ROWS), F32), ((1, ROWS), F32)],
        total, from_core, from_y, from_cross, emb_t, emb_state.reshape(1, ROWS),
    )
    gw = jnp.sum(gw.astype(F32), axis=0).astype(BF)
    gw = jnp.broadcast_to(gw[None], (XY, RELS, D))
    gw = lax.all_to_all(gw, ("x", "yh"), split_axis=0, concat_axis=0, tiled=True)
    (rel_new,) = call(update_kernel, "svv", [((RELS, D), F32)], rel_state, gw, rel_weight)
    return (new_t.T, fresh.reshape(ROWS), rel_new)


def solution(mesh):
    fine = Mesh(mesh.devices.reshape(4, 2, Z, N_REL), ("x", "yh", "z", "rel"))
    in_specs = (
        P(DOM, None),
        P(DOM),
        P("rel", None),
        P("rel"),
        P(),
        P("rel", DOM),
        P("rel", DOM),
        P("rel", DOM),
        P("rel", DOM),
        P("rel", DOM),
        P(DOM),
        P("rel", DOM),
        P("rel", DOM),
        P("rel", DOM),
    )
    out_specs = (P(DOM, None), P(DOM), P("rel", None))
    return jax.shard_map(
        body, mesh=fine, in_specs=in_specs, out_specs=out_specs, check_vma=False
    )
```

```python
import jax
import jax.numpy as jnp
from jax import lax
from jax.experimental import pallas as pl
from jax.experimental.pallas import tpu as pltpu
from jax.sharding import Mesh
from jax.sharding import PartitionSpec as P

step_rate = 0.25

D = 400
TILE = 128
ROWS = 256
HALF = ROWS // 2
BND = 128
E_ROWS = 512
B_ROWS = 256
A_ROWS = E_ROWS + B_ROWS
E_TILES = E_ROWS // TILE
B_TILES = B_ROWS // TILE
A_TILES = E_TILES + B_TILES
N_REL = 4
RELS = 8
NEG_TILES = 8
NEG = NEG_TILES * TILE
INFO = 16
SENT = D + INFO
RIM_INFO = 8
RIM = D + RIM_INFO
RIM_WIDTH = BND + B_ROWS

LIMIT = 24 << 20

BF = jnp.bfloat16
F32 = jnp.float32
DOM = ("x", "yh", "z")
Z = 16
XY = 8


def vmem():
    return pl.BlockSpec(memory_space=pltpu.VMEM)


def smem():
    return pl.BlockSpec(memory_space=pltpu.SMEM)


def call(kernel, ins, outs, *args):
    return pl.pallas_call(
        kernel,
        in_specs=[smem() if kind == "s" else vmem() for kind in ins],
        out_specs=[vmem() for _ in outs],
        out_shape=[jax.ShapeDtypeStruct(shape, dtype) for shape, dtype in outs],
        compiler_params=pltpu.CompilerParams(vmem_limit_bytes=LIMIT),
    )(*args)


def mm(a, b, dims):
    return lax.dot_general(a, b, (dims, ((), ())), preferred_element_type=F32)


NN = ((1,), (0,))
NT = ((1,), (1,))
TN = ((0,), (0,))


def two(values):
    high = values.astype(BF)
    return high, (values - high.astype(F32)).astype(BF)


def hits(count, ids):
    return lax.broadcasted_iota(jnp.int32, (count, ids.shape[1]), 0) == ids


def ones(mask):
    return mask.astype(F32).astype(BF)


def stacked(count, width, lists):
    row = lax.broadcasted_iota(jnp.int32, (count, width), 0)
    block = jnp.zeros((count, width), F32)
    for k, values in enumerate(lists):
        values = values.astype(F32)
        if values.shape[1] < width:
            values = jnp.concatenate(
                [values, jnp.zeros((1, width - values.shape[1]), F32)], axis=1
            )
        block = jnp.where(row == k, values, block)
    return block.astype(BF)


def relations(ids):
    spread = [jnp.broadcast_to(ident, (1, TILE)).astype(jnp.int32) for ident in ids]
    return ones(hits(RELS, jnp.concatenate(spread, axis=1)))


def weights(relw, ids):
    lane = lax.broadcasted_iota(jnp.int32, (RELS, TILE), 1)
    row = lax.broadcasted_iota(jnp.int32, (RELS, TILE), 0)
    chosen = jnp.zeros((RELS, TILE), F32)
    for t, ident in enumerate(ids):
        chosen = jnp.where((lane == t) & (row == ident), 1.0, chosen)
    chosen = chosen.astype(BF)
    high = relw.astype(BF)
    rest = relw - high.astype(F32)
    middle = rest.astype(BF)
    low = (rest - middle.astype(F32)).astype(BF)
    return (mm(high, chosen, TN) + mm(middle, chosen, TN)) + mm(low, chosen, TN)


def scaled(rows, columns):
    return jnp.concatenate(
        [
            rows[:, t * TILE : (t + 1) * TILE] * columns[:, t : t + 1]
            for t in range(rows.shape[1] // TILE)
        ],
        axis=1,
    )


def tile_ids(tile_ref, band_ref):
    return [tile_ref[0, t] for t in range(E_TILES)], [band_ref[0, t] for t in range(B_TILES)]


def second_count(neg_ref):
    second = neg_ref[0, 0]
    for t in range(1, NEG_TILES):
        second = second + neg_ref[0, t]
    return second


def start_kernel(
    core_ref, tile_ref, band_ref, live_ref, neg_ref, emb_ref, relw_ref, src_ref, dst_ref, bsrc_ref,
    bdst_ref, bound_ref,
    part_ref, up_ref, down_ref, brows_ref,
):
    high, low = two(emb_ref[...])
    part_ref[:D, :] = jnp.where(core_ref[0] == 0, high[:, :HALF], high[:, HALF:])
    edge_ids, band_ids = tile_ids(tile_ref, band_ref)
    lane = lax.broadcasted_iota(jnp.int32, (1, TILE), 1)
    scalars = jnp.zeros((1, TILE), F32)
    for k, number in enumerate([*edge_ids, *band_ids, live_ref[0, 0], second_count(neg_ref)]):
        scalars = jnp.where(lane == k, number.astype(F32), scalars)
    lists = []
    for ref in (src_ref, bsrc_ref, dst_ref):
        lists += [ref[:, k : k + TILE] for k in range(0, ref.shape[1], TILE)]
    part_ref[D:, :] = stacked(INFO, TILE, [*lists, scalars])
    rim = mm(high, ones(hits(ROWS, bound_ref[...])), NN).astype(BF)
    up_ref[:D, :BND] = rim[:, BND:]
    down_ref[:D, :BND] = rim[:, :BND]
    pick = ones(hits(ROWS, bsrc_ref[...]))
    rows = mm(high, pick, NN) + mm(low, pick, NN)
    brows_ref[...] = rows
    q = scaled(rows, weights(relw_ref[...], band_ids)).astype(BF)
    info = stacked(RIM_INFO, RIM_WIDTH, [bdst_ref[...]])
    for ref in (up_ref, down_ref):
        ref[:D, BND:] = q
        ref[D:, :] = info


def pull(scores, hit):
    pos = jnp.sum(jnp.where(hit, scores, 0.0), axis=0, keepdims=True)
    return jnp.where(hit, -jax.nn.sigmoid(-pos), 0.0)


def source_kernel(
    tile_ref, band_ref, emb_ref, relw_ref, src_ref, bdst_ref, bound_ref, own_up_ref, own_down_ref,
    low_ref, high_ref,
    q_ref, rows_ref, dqb_ref, back_ref,
):
    high, low = two(emb_ref[...])
    pick = ones(hits(ROWS, src_ref[...]))
    rows = mm(high, pick, NN) + mm(low, pick, NN)
    rows_ref[...] = rows
    edge_ids, _ = tile_ids(tile_ref, band_ref)
    q_ref[:, :E_ROWS] = scaled(rows, weights(relw_ref[...], edge_ids)).astype(BF)
    qb = own_up_ref[:D, BND:]
    q_ref[:, E_ROWS:] = qb
    near = jnp.concatenate([low_ref[:D, :BND], high_ref[:D, :BND]], axis=1)
    dqb_ref[...] = mm(near, pull(mm(near, qb, TN), hits(2 * BND, bdst_ref[...])).astype(BF), NN)
    grads = []
    for got_ref, mine_ref, shift in ((low_ref, own_down_ref, BND), (high_ref, own_up_ref, 0)):
        qn = got_ref[:D, BND:]
        ids = got_ref[D:, :].astype(F32)[:1, :B_ROWS].astype(jnp.int32) - shift
        grads.append(mm(qn, pull(mm(mine_ref[:D, :BND], qn, TN), hits(BND, ids)).astype(BF), NT))
    grads = jnp.concatenate(grads, axis=1).astype(BF)
    back_ref[...] = mm(grads, ones(hits(ROWS, bound_ref[...])), NT)


def coefficients(scores, dst, live, second):
    edge = lax.broadcasted_iota(jnp.int32, (1, A_ROWS), 1)
    valid = jnp.where((edge < live * TILE) | (edge >= E_ROWS), 1.0, 0.0)
    counts = jnp.where(
        lax.broadcasted_iota(jnp.int32, (ROWS, 1), 0) < TILE, NEG_TILES - second, second
    )
    dneg = (jax.nn.sigmoid(scores) * (valid / NEG)).astype(BF).astype(F32) * counts
    positive = pull(scores[:, :E_ROWS], hits(ROWS, dst)) * valid[:, :E_ROWS]
    return jnp.concatenate([dneg[:, :E_ROWS] + positive, dneg[:, E_ROWS:]], axis=1).astype(BF)


def far_block(core_ref, got_ref, other_ref):
    got, other = got_ref[:D, :], other_ref[:D, :]
    first = core_ref[0] == 0
    return jnp.concatenate([jnp.where(first, got, other), jnp.where(first, other, got)], axis=1)


def relation_kernel(
    core_ref, tile_ref, band_ref, live_ref, neg_ref, got_ref, other_ref, q_ref, rows_ref, brows_ref,
    dqb_ref, relw_ref, dst_ref,
    gw_ref, step_ref,
):
    far = far_block(core_ref, got_ref, other_ref)
    scores = mm(far, q_ref[...], TN)
    coef = coefficients(
        scores, dst_ref[...], live_ref[0, 0], second_count(neg_ref).astype(F32)
    )
    edge_ids, band_ids = tile_ids(tile_ref, band_ref)
    chosen = relations(edge_ids + band_ids)
    dq = mm(far, coef, NN)
    dq_band = dq[:, E_ROWS:] + dqb_ref[...]
    first = (dq[:, :E_ROWS] * rows_ref[...]).astype(BF)
    second = (dq_band * brows_ref[...]).astype(BF)
    gw = mm(chosen[:, :E_ROWS], first, NT) + mm(chosen[:, E_ROWS:], second, NT)
    gw = gw.astype(BF)
    for k in range(Z):
        gw_ref[k, :, :] = gw
    columns = weights(relw_ref[...], edge_ids + band_ids)
    step_ref[:, :E_ROWS] = scaled(dq[:, :E_ROWS], columns).astype(BF)
    step_ref[:, E_ROWS:] = scaled(dq_band, columns[:, E_TILES:A_TILES]).astype(BF)


def partner_kernel(
    core_ref, got_ref, other_ref, emb_ref, relw_ref, step_ref, src_ref, bsrc_ref, back_ref,
    total_ref,
):
    far = far_block(core_ref, got_ref, other_ref)
    info = got_ref[D:, :].astype(F32)
    ids = jnp.concatenate([info[k : k + 1, :] for k in range(10)], axis=1).astype(jnp.int32)
    scalars = info[10:11, :]
    columns = weights(relw_ref[...], [scalars[:, t : t + 1].astype(jnp.int32) for t in range(A_TILES)])
    q = scaled(mm(far, ones(hits(ROWS, ids[:, :A_ROWS])), NN), columns).astype(BF)
    scores = mm(emb_ref[...].astype(BF), q, TN)
    coef = coefficients(
        scores,
        ids[:, A_ROWS:],
        scalars[:, A_TILES : A_TILES + 1].astype(jnp.int32),
        scalars[:, A_TILES + 1 : A_TILES + 2],
    )
    pick = jnp.concatenate([ones(hits(ROWS, src_ref[...])), ones(hits(ROWS, bsrc_ref[...]))], axis=1)
    total = back_ref[...] + mm(step_ref[...], pick, NT) + mm(q, coef, NT)
    total_ref[...] = total.astype(BF)


def final_kernel(own_ref, core_ref, far_ref, cross_ref, emb_ref, state_ref, new_ref, fresh_ref):
    near = own_ref[...].astype(F32) + core_ref[...].astype(F32)
    grad = near + (far_ref[...].astype(F32) + cross_ref[...].astype(F32))
    fresh = state_ref[...] + jnp.sum(grad * grad, axis=0, keepdims=True) / D
    fresh_ref[...] = fresh
    new_ref[...] = emb_ref[...] - step_rate * grad / jnp.sqrt(fresh)


def swap(axes, size, number, work):
    def branch(k):
        def run(moved, *args):
            if k:
                moved = lax.ppermute(moved, axes, [(i, i ^ k) for i in range(size)])
            return (moved, *work(*args))

        return run

    return lambda *args: lax.switch(number, [branch(k) for k in range(size)], *args)


def trade(values, bit):
    return lax.ppermute(values, "rel", [(i, i ^ bit) for i in range(N_REL)])


def body(
    emb, emb_state, rel_weight, rel_state, swap_mask, src_rows, dst_rows, tile_rel, live_tiles,
    neg_tiles, bound_rows, band_src, band_dst, band_rel,
):
    mask = swap_mask[0]
    bound = bound_rows.reshape(1, 2 * BND)
    core = lax.bitwise_and(lax.axis_index("rel").astype(jnp.int32), 1).reshape(1)
    count = lax.axis_size(DOM)
    emb_t = emb.T
    part, to_up, to_down, band_rows = call(
        start_kernel,
        "sssssvvvvvvv",
        [((SENT, HALF), BF), ((RIM, RIM_WIDTH), BF), ((RIM, RIM_WIDTH), BF), ((D, B_ROWS), F32)],
        core, tile_rel, band_rel, live_tiles, neg_tiles, emb_t, rel_weight, src_rows, dst_rows,
        band_src, band_dst, bound,
    )
    from_low = lax.ppermute(to_up, DOM, [(i, i + 1) for i in range(count - 1)])
    from_high = lax.ppermute(to_down, DOM, [(i + 1, i) for i in range(count - 1)])
    (got,) = swap("z", Z, lax.bitwise_and(mask, 15), lambda: ())(part)

    def sources(*args):
        return call(
            source_kernel,
            "ssvvvvvvvvv",
            [((D, A_ROWS), BF), ((D, E_ROWS), F32), ((D, B_ROWS), F32), ((D, ROWS), F32)],
            *args,
        )

    along_xy = swap(("x", "yh"), XY, lax.shift_right_logical(mask, 4), sources)
    got, q, rows, dq_band, back = along_xy(
        got, tile_rel, band_rel, emb_t, rel_weight, src_rows, band_dst, bound, to_up, to_down,
        from_low, from_high,
    )
    other_half = trade(got, 1)
    gw, step = call(
        relation_kernel,
        "sssssvvvvvvvv",
        [((Z, RELS, D), BF), ((D, A_ROWS), BF)],
        core, tile_rel, band_rel, live_tiles, neg_tiles, got, other_half, q, rows, band_rows,
        dq_band, rel_weight, dst_rows,
    )
    gw = lax.all_to_all(gw, "z", split_axis=0, concat_axis=0, tiled=True)
    (total,) = call(
        partner_kernel,
        "svvvvvvvv",
        [((D, ROWS), BF)],
        core, got, other_half, emb_t, rel_weight, step, src_rows,
        band_src, back,
    )
    from_cross = trade(total, 3)
    from_y = trade(total, 2)
    from_core = trade(total, 1)
    new_t, fresh = call(
        final_kernel,
        "vvvvvv",
        [((D, ROWS), F32), ((1, ROWS), F32)],
        total, from_core, from_y, from_cross, emb_t, emb_state.reshape(1, ROWS),
    )
    gw = jnp.sum(gw.astype(F32), axis=0).astype(BF)
    gw = jnp.broadcast_to(gw[None], (XY, RELS, D))
    gw = lax.all_to_all(gw, ("x", "yh"), split_axis=0, concat_axis=0, tiled=True)
    gw = jnp.sum(gw.astype(F32), axis=0)
    rel_new = rel_weight - step_rate * gw / jnp.sqrt(rel_state + jnp.mean(gw * gw, axis=1))[:, None]
    return (new_t.T, fresh.reshape(ROWS), rel_new)


def solution(mesh):
    fine = Mesh(mesh.devices.reshape(4, 2, Z, N_REL), ("x", "yh", "z", "rel"))
    in_specs = (
        P(DOM, None),
        P(DOM),
        P("rel", None),
        P("rel"),
        P(),
        P("rel", DOM),
        P("rel", DOM),
        P("rel", DOM),
        P("rel", DOM),
        P("rel", DOM),
        P(DOM),
        P("rel", DOM),
        P("rel", DOM),
        P("rel", DOM),
    )
    out_specs = (P(DOM, None), P(DOM), P("rel", None))
    return jax.shard_map(
        body, mesh=fine, in_specs=in_specs, out_specs=out_specs, check_vma=False
    )
```

```python
import jax
import jax.numpy as jnp
from jax import lax
from jax.experimental import pallas as pl
from jax.experimental.pallas import tpu as pltpu
from jax.sharding import Mesh
from jax.sharding import PartitionSpec as P

step_rate = 0.25

D = 400
TILE = 128
ROWS = 256
HALF = ROWS // 2
BND = 128
E_ROWS = 512
B_ROWS = 256
A_ROWS = E_ROWS + B_ROWS
E_TILES = E_ROWS // TILE
B_TILES = B_ROWS // TILE
A_TILES = E_TILES + B_TILES
N_REL = 4
RELS = 8
NEG_TILES = 8
NEG = NEG_TILES * TILE
INFO = 16
SENT = D + INFO
RIM_INFO = 8
RIM = D + RIM_INFO
RIM_WIDTH = BND + B_ROWS

LIMIT = 24 << 20

BF = jnp.bfloat16
F32 = jnp.float32
XY = ("x", "yh")
ZZ = ("zh", "zl")
DOM = (*XY, *ZZ)
Z = 16
FIRST = 8
SECOND = 16


def vmem():
    return pl.BlockSpec(memory_space=pltpu.VMEM)


def smem():
    return pl.BlockSpec(memory_space=pltpu.SMEM)


def call(kernel, ins, outs, *args):
    return pl.pallas_call(
        kernel,
        in_specs=[smem() if kind == "s" else vmem() for kind in ins],
        out_specs=[vmem() for _ in outs],
        out_shape=[jax.ShapeDtypeStruct(shape, dtype) for shape, dtype in outs],
        compiler_params=pltpu.CompilerParams(vmem_limit_bytes=LIMIT),
    )(*args)


def mm(a, b, dims):
    return lax.dot_general(a, b, (dims, ((), ())), preferred_element_type=F32)


NN = ((1,), (0,))
NT = ((1,), (1,))
TN = ((0,), (0,))


def two(values):
    high = values.astype(BF)
    return high, (values - high.astype(F32)).astype(BF)


def hits(count, ids):
    return lax.broadcasted_iota(jnp.int32, (count, ids.shape[1]), 0) == ids


def ones(mask):
    return mask.astype(F32).astype(BF)


def stacked(count, width, lists):
    row = lax.broadcasted_iota(jnp.int32, (count, width), 0)
    block = jnp.zeros((count, width), F32)
    for k, values in enumerate(lists):
        values = values.astype(F32)
        if values.shape[1] < width:
            values = jnp.concatenate(
                [values, jnp.zeros((1, width - values.shape[1]), F32)], axis=1
            )
        block = jnp.where(row == k, values, block)
    return block.astype(BF)


def relations(ids):
    spread = [jnp.broadcast_to(ident, (1, TILE)).astype(jnp.int32) for ident in ids]
    return ones(hits(RELS, jnp.concatenate(spread, axis=1)))


def weights(relw, ids):
    lane = lax.broadcasted_iota(jnp.int32, (RELS, TILE), 1)
    row = lax.broadcasted_iota(jnp.int32, (RELS, TILE), 0)
    chosen = jnp.zeros((RELS, TILE), F32)
    for t, ident in enumerate(ids):
        chosen = jnp.where((lane == t) & (row == ident), 1.0, chosen)
    chosen = chosen.astype(BF)
    high = relw.astype(BF)
    rest = relw - high.astype(F32)
    middle = rest.astype(BF)
    low = (rest - middle.astype(F32)).astype(BF)
    return (mm(high, chosen, TN) + mm(middle, chosen, TN)) + mm(low, chosen, TN)


def scaled(rows, columns):
    return jnp.concatenate(
        [
            rows[:, t * TILE : (t + 1) * TILE] * columns[:, t : t + 1]
            for t in range(rows.shape[1] // TILE)
        ],
        axis=1,
    )


def number(info, k):
    return info[:, k : k + 1].astype(jnp.int32)


def tile_numbers(info):
    return [number(info, k) for k in range(A_TILES)]


def same_order(core, own, other):
    first = core == 0
    return jnp.concatenate([jnp.where(first, own, other), jnp.where(first, other, own)], axis=1)


def start_kernel(
    core_ref, tile_ref, band_ref, live_ref, neg_ref, emb_ref, relw_ref, src_ref, dst_ref, bsrc_ref,
    bdst_ref, bound_ref,
    part_ref, up_ref, down_ref, brows_ref, info_ref,
):
    high, low = two(emb_ref[...])
    part_ref[:D, :] = jnp.where(core_ref[0] == 0, high[:, :HALF], high[:, HALF:])
    numbers = [tile_ref[0, t] for t in range(E_TILES)] + [band_ref[0, t] for t in range(B_TILES)]
    second = neg_ref[0, 0]
    for t in range(1, NEG_TILES):
        second = second + neg_ref[0, t]
    lane = lax.broadcasted_iota(jnp.int32, (1, TILE), 1)
    scalars = jnp.zeros((1, TILE), F32)
    for k, value in enumerate([*numbers, live_ref[0, 0], second, core_ref[0]]):
        scalars = jnp.where(lane == k, value.astype(F32), scalars)
    info_ref[...] = jnp.broadcast_to(scalars, (RELS, TILE))
    lists = []
    for ref in (src_ref, bsrc_ref, dst_ref):
        lists += [ref[:, k : k + TILE] for k in range(0, ref.shape[1], TILE)]
    part_ref[D:, :] = stacked(INFO, TILE, [*lists, scalars])
    rim = mm(high, ones(hits(ROWS, bound_ref[...])), NN).astype(BF)
    up_ref[:D, :BND] = rim[:, BND:]
    down_ref[:D, :BND] = rim[:, :BND]
    pick = ones(hits(ROWS, bsrc_ref[...]))
    rows = mm(high, pick, NN) + mm(low, pick, NN)
    brows_ref[...] = rows
    q = scaled(rows, weights(relw_ref[...], numbers[E_TILES:])).astype(BF)
    info = stacked(RIM_INFO, RIM_WIDTH, [bdst_ref[...]])
    for ref in (up_ref, down_ref):
        ref[:D, BND:] = q
        ref[D:, :] = info


def pull(scores, hit):
    pos = jnp.sum(jnp.where(hit, scores, 0.0), axis=0, keepdims=True)
    return jnp.where(hit, -jax.nn.sigmoid(-pos), 0.0)


def source_kernel(
    info_ref, emb_ref, relw_ref, src_ref, bdst_ref, bound_ref, own_up_ref, own_down_ref, low_ref,
    high_ref,
    q_ref, rows_ref, dqb_ref, back_ref,
):
    high, low = two(emb_ref[...])
    pick = ones(hits(ROWS, src_ref[...]))
    rows = mm(high, pick, NN) + mm(low, pick, NN)
    rows_ref[...] = rows
    columns = weights(relw_ref[...], tile_numbers(info_ref[:1, :]))
    q_ref[:, :E_ROWS] = scaled(rows, columns).astype(BF)
    qb = own_up_ref[:D, BND:]
    q_ref[:, E_ROWS:] = qb
    near = jnp.concatenate([low_ref[:D, :BND], high_ref[:D, :BND]], axis=1)
    first, second = two(pull(mm(near, qb, TN), hits(2 * BND, bdst_ref[...])))
    dqb_ref[...] = mm(near, first, NN) + mm(near, second, NN)
    grads = []
    for got_ref, mine_ref, shift in ((low_ref, own_down_ref, BND), (high_ref, own_up_ref, 0)):
        qn = got_ref[:D, BND:]
        ids = got_ref[D:, :].astype(F32)[:1, :B_ROWS].astype(jnp.int32) - shift
        first, second = two(pull(mm(mine_ref[:D, :BND], qn, TN), hits(BND, ids)))
        grads.append(mm(qn, first, NT) + mm(qn, second, NT))
    first, second = two(jnp.concatenate(grads, axis=1))
    pick = ones(hits(ROWS, bound_ref[...]))
    back_ref[...] = mm(first, pick, NT) + mm(second, pick, NT)


def coefficients(scores, dst, live, second):
    edge = lax.broadcasted_iota(jnp.int32, (1, A_ROWS), 1)
    valid = jnp.where((edge < live * TILE) | (edge >= E_ROWS), 1.0, 0.0)
    counts = jnp.where(
        lax.broadcasted_iota(jnp.int32, (ROWS, 1), 0) < TILE, NEG_TILES - second, second
    )
    dneg = (jax.nn.sigmoid(scores) * (valid / NEG)).astype(BF).astype(F32) * counts
    positive = pull(scores[:, :E_ROWS], hits(ROWS, dst)) * valid[:, :E_ROWS]
    high, low = two(dneg[:, :E_ROWS] + positive)
    return jnp.concatenate([high, dneg[:, E_ROWS:].astype(BF)], axis=1), low


def relation_kernel(
    info_ref, got_ref, other_ref, q_ref, rows_ref, brows_ref, dqb_ref, relw_ref, dst_ref,
    gw_ref, step_ref,
):
    info = info_ref[:1, :]
    ids = tile_numbers(info)
    far = same_order(number(info, A_TILES + 2), got_ref[:D, :], other_ref[:D, :])
    scores = mm(far, q_ref[...], TN)
    coef, rest = coefficients(
        scores, dst_ref[...], number(info, A_TILES), info[:, A_TILES + 1 : A_TILES + 2]
    )
    chosen = relations(ids)
    dq = mm(far, coef, NN)
    dq_edge = dq[:, :E_ROWS] + mm(far, rest, NN)
    dq_band = dq[:, E_ROWS:] + dqb_ref[...]
    first = (dq_edge * rows_ref[...]).astype(BF)
    second = (dq_band * brows_ref[...]).astype(BF)
    gw = mm(chosen[:, :E_ROWS], first, NT) + mm(chosen[:, E_ROWS:], second, NT)
    gw = gw.astype(BF)
    for k in range(FIRST):
        gw_ref[k, :, :] = gw
    columns = weights(relw_ref[...], ids)
    step_ref[:, :E_ROWS] = scaled(dq_edge, columns).astype(BF)
    step_ref[:, E_ROWS:] = scaled(dq_band, columns[:, E_TILES:A_TILES]).astype(BF)


def partner_kernel(
    info_ref, got_ref, other_ref, emb_ref, relw_ref, step_ref, src_ref, bsrc_ref, back_ref,
    total_ref,
):
    core = number(info_ref[:1, :], A_TILES + 2)
    far = same_order(core, got_ref[:D, :], other_ref[:D, :])
    info = got_ref[D:, :].astype(F32)
    ids = jnp.concatenate([info[k : k + 1, :] for k in range(10)], axis=1).astype(jnp.int32)
    scalars = info[10:11, :]
    columns = weights(relw_ref[...], tile_numbers(scalars))
    q = scaled(mm(far, ones(hits(ROWS, ids[:, :A_ROWS])), NN), columns).astype(BF)
    scores = mm(emb_ref[...].astype(BF), q, TN)
    coef, rest = coefficients(
        scores, ids[:, A_ROWS:], number(scalars, A_TILES), scalars[:, A_TILES + 1 : A_TILES + 2]
    )
    pick = jnp.concatenate([ones(hits(ROWS, src_ref[...])), ones(hits(ROWS, bsrc_ref[...]))], axis=1)
    total = back_ref[...] + mm(step_ref[...], pick, NT) + mm(q, coef, NT)
    total = total + mm(q[:, :E_ROWS], rest, NT)
    total_ref[...] = total.astype(BF)


def final_kernel(own_ref, core_ref, far_ref, cross_ref, emb_ref, state_ref, new_ref, fresh_ref):
    near = own_ref[...].astype(F32) + core_ref[...].astype(F32)
    grad = near + (far_ref[...].astype(F32) + cross_ref[...].astype(F32))
    fresh = state_ref[...] + jnp.sum(grad * grad, axis=0, keepdims=True) / D
    fresh_ref[...] = fresh
    new_ref[...] = emb_ref[...] - step_rate * grad / jnp.sqrt(fresh)


def swap(axes, size, number, work):
    def branch(k):
        def run(moved, *args):
            if k:
                moved = lax.ppermute(moved, axes, [(i, i ^ k) for i in range(size)])
            return (moved, *work(*args))

        return run

    return lambda *args: lax.switch(number, [branch(k) for k in range(size)], *args)


def trade(values, bit):
    return lax.ppermute(values, "rel", [(i, i ^ bit) for i in range(N_REL)])


def body(
    emb, emb_state, rel_weight, rel_state, swap_mask, src_rows, dst_rows, tile_rel, live_tiles,
    neg_tiles, bound_rows, band_src, band_dst, band_rel,
):
    mask = swap_mask[0]
    bound = bound_rows.reshape(1, 2 * BND)
    core = lax.bitwise_and(lax.axis_index("rel").astype(jnp.int32), 1).reshape(1)
    count = lax.axis_size(DOM)
    emb_t = emb.T
    part, to_up, to_down, band_rows, info = call(
        start_kernel,
        "sssssvvvvvvv",
        [
            ((SENT, HALF), BF),
            ((RIM, RIM_WIDTH), BF),
            ((RIM, RIM_WIDTH), BF),
            ((D, B_ROWS), F32),
            ((RELS, TILE), F32),
        ],
        core, tile_rel, band_rel, live_tiles, neg_tiles, emb_t, rel_weight, src_rows, dst_rows,
        band_src, band_dst, bound,
    )
    from_low = lax.ppermute(to_up, DOM, [(i, i + 1) for i in range(count - 1)])
    from_high = lax.ppermute(to_down, DOM, [(i + 1, i) for i in range(count - 1)])
    (got,) = swap(ZZ, Z, lax.bitwise_and(mask, 15), lambda: ())(part)

    def sources(*args):
        return call(
            source_kernel,
            "vvvvvvvvvv",
            [((D, A_ROWS), BF), ((D, E_ROWS), F32), ((D, B_ROWS), F32), ((D, ROWS), F32)],
            *args,
        )

    along_xy = swap(XY, 8, lax.shift_right_logical(mask, 4), sources)
    got, q, rows, dq_band, back = along_xy(
        got, info, emb_t, rel_weight, src_rows, band_dst, bound, to_up, to_down, from_low, from_high
    )
    other_half = trade(got, 1)
    gw, step = call(
        relation_kernel,
        "vvvvvvvvv",
        [((FIRST, RELS, D), BF), ((D, A_ROWS), BF)],
        info, got, other_half, q, rows, band_rows, dq_band, rel_weight, dst_rows,
    )
    gw = lax.all_to_all(gw, "zh", split_axis=0, concat_axis=0, tiled=True)
    (total,) = call(
        partner_kernel,
        "vvvvvvvvv",
        [((D, ROWS), BF)],
        info, got, other_half, emb_t, rel_weight, step, src_rows,
        band_src, back,
    )
    from_cross = trade(total, 3)
    from_y = trade(total, 2)
    from_core = trade(total, 1)
    new_t, fresh = call(
        final_kernel,
        "vvvvvv",
        [((D, ROWS), F32), ((1, ROWS), F32)],
        total, from_core, from_y, from_cross, emb_t, emb_state.reshape(1, ROWS),
    )
    gw = jnp.sum(gw.astype(F32), axis=0).astype(BF)
    gw = jnp.broadcast_to(gw[None], (SECOND, RELS, D))
    gw = lax.all_to_all(gw, (*XY, "zl"), split_axis=0, concat_axis=0, tiled=True)
    gw = jnp.sum(gw.astype(F32), axis=0)
    rel_new = rel_weight - step_rate * gw / jnp.sqrt(rel_state + jnp.mean(gw * gw, axis=1))[:, None]
    return (new_t.T, fresh.reshape(ROWS), rel_new)


def solution(mesh):
    fine = Mesh(mesh.devices.reshape(4, 2, 8, 2, N_REL), (*DOM, "rel"))
    in_specs = (
        P(DOM, None),
        P(DOM),
        P("rel", None),
        P("rel"),
        P(),
        P("rel", DOM),
        P("rel", DOM),
        P("rel", DOM),
        P("rel", DOM),
        P("rel", DOM),
        P(DOM),
        P("rel", DOM),
        P("rel", DOM),
        P("rel", DOM),
    )
    out_specs = (P(DOM, None), P(DOM), P("rel", None))
    return jax.shard_map(
        body, mesh=fine, in_specs=in_specs, out_specs=out_specs, check_vma=False
    )
```

```python
import jax
import jax.numpy as jnp
from jax import lax
from jax.experimental import pallas as pl
from jax.experimental.pallas import tpu as pltpu
from jax.sharding import Mesh
from jax.sharding import PartitionSpec as P

step_rate = 0.25

D = 400
TILE = 128
ROWS = 256
HALF = ROWS // 2
BND = 128
E_ROWS = 512
B_ROWS = 256
A_ROWS = E_ROWS + B_ROWS
E_TILES = E_ROWS // TILE
B_TILES = B_ROWS // TILE
A_TILES = E_TILES + B_TILES
N_REL = 4
RELS = 8
NEG_TILES = 8
NEG = NEG_TILES * TILE
INFO = 16
SENT = D + INFO
RIM_INFO = 8
RIM = D + RIM_INFO
RIM_WIDTH = BND + B_ROWS

LIMIT = 24 << 20
WIDE = 56 << 20

BF = jnp.bfloat16
F32 = jnp.float32
XY = ("x", "yh")
ZZ = ("zh", "zl")
DOM = (*XY, *ZZ)
Z = 16
FIRST = 16
SECOND = 8


def vmem():
    return pl.BlockSpec(memory_space=pltpu.VMEM)


def smem():
    return pl.BlockSpec(memory_space=pltpu.SMEM)


def call(kernel, ins, outs, *args, limit=LIMIT):
    return pl.pallas_call(
        kernel,
        in_specs=[smem() if kind == "s" else vmem() for kind in ins],
        out_specs=[vmem() for _ in outs],
        out_shape=[jax.ShapeDtypeStruct(shape, dtype) for shape, dtype in outs],
        compiler_params=pltpu.CompilerParams(vmem_limit_bytes=limit),
    )(*args)


def mm(a, b, dims):
    return lax.dot_general(a, b, (dims, ((), ())), preferred_element_type=F32)


NN = ((1,), (0,))
NT = ((1,), (1,))
TN = ((0,), (0,))


def two(values):
    high = values.astype(BF)
    return high, (values - high.astype(F32)).astype(BF)


def hits(count, ids):
    return lax.broadcasted_iota(jnp.int32, (count, ids.shape[1]), 0) == ids


def ones(mask):
    return mask.astype(F32).astype(BF)


def stacked(count, width, lists):
    row = lax.broadcasted_iota(jnp.int32, (count, width), 0)
    block = jnp.zeros((count, width), F32)
    for k, values in enumerate(lists):
        values = values.astype(F32)
        if values.shape[1] < width:
            values = jnp.concatenate(
                [values, jnp.zeros((1, width - values.shape[1]), F32)], axis=1
            )
        block = jnp.where(row == k, values, block)
    return block.astype(BF)


def relations(ids):
    spread = [jnp.broadcast_to(ident, (1, TILE)).astype(jnp.int32) for ident in ids]
    return ones(hits(RELS, jnp.concatenate(spread, axis=1)))


def weights(relw, ids):
    lane = lax.broadcasted_iota(jnp.int32, (RELS, TILE), 1)
    row = lax.broadcasted_iota(jnp.int32, (RELS, TILE), 0)
    chosen = jnp.zeros((RELS, TILE), F32)
    for t, ident in enumerate(ids):
        chosen = jnp.where((lane == t) & (row == ident), 1.0, chosen)
    chosen = chosen.astype(BF)
    high = relw.astype(BF)
    rest = relw - high.astype(F32)
    middle = rest.astype(BF)
    low = (rest - middle.astype(F32)).astype(BF)
    return (mm(high, chosen, TN) + mm(middle, chosen, TN)) + mm(low, chosen, TN)


def scaled(rows, columns):
    return jnp.concatenate(
        [
            rows[:, t * TILE : (t + 1) * TILE] * columns[:, t : t + 1]
            for t in range(rows.shape[1] // TILE)
        ],
        axis=1,
    )


def number(info, k):
    return info[:, k : k + 1].astype(jnp.int32)


def tile_numbers(info):
    return [number(info, k) for k in range(A_TILES)]


def same_order(core, own, other):
    first = core == 0
    return jnp.concatenate([jnp.where(first, own, other), jnp.where(first, other, own)], axis=1)


def start_kernel(
    core_ref, tile_ref, band_ref, live_ref, neg_ref, emb_ref, relw_ref, src_ref, dst_ref, bsrc_ref,
    bdst_ref, bound_ref,
    part_ref, up_ref, down_ref, brows_ref, info_ref,
):
    high, low = two(emb_ref[...])
    part_ref[:D, :] = jnp.where(core_ref[0] == 0, high[:, :HALF], high[:, HALF:])
    numbers = [tile_ref[0, t] for t in range(E_TILES)] + [band_ref[0, t] for t in range(B_TILES)]
    second = neg_ref[0, 0]
    for t in range(1, NEG_TILES):
        second = second + neg_ref[0, t]
    lane = lax.broadcasted_iota(jnp.int32, (1, TILE), 1)
    scalars = jnp.zeros((1, TILE), F32)
    for k, value in enumerate([*numbers, live_ref[0, 0], second, core_ref[0]]):
        scalars = jnp.where(lane == k, value.astype(F32), scalars)
    info_ref[...] = jnp.broadcast_to(scalars, (RELS, TILE))
    lists = []
    for ref in (src_ref, bsrc_ref, dst_ref):
        lists += [ref[:, k : k + TILE] for k in range(0, ref.shape[1], TILE)]
    part_ref[D:, :] = stacked(INFO, TILE, [*lists, scalars])
    rim = mm(high, ones(hits(ROWS, bound_ref[...])), NN).astype(BF)
    up_ref[:D, :BND] = rim[:, BND:]
    down_ref[:D, :BND] = rim[:, :BND]
    pick = ones(hits(ROWS, bsrc_ref[...]))
    rows = mm(high, pick, NN) + mm(low, pick, NN)
    brows_ref[...] = rows
    q = scaled(rows, weights(relw_ref[...], numbers[E_TILES:])).astype(BF)
    info = stacked(RIM_INFO, RIM_WIDTH, [bdst_ref[...]])
    for ref in (up_ref, down_ref):
        ref[:D, BND:] = q
        ref[D:, :] = info


def pull(scores, hit):
    pos = jnp.sum(jnp.where(hit, scores, 0.0), axis=0, keepdims=True)
    return jnp.where(hit, -jax.nn.sigmoid(-pos), 0.0)


def source_kernel(
    info_ref, emb_ref, relw_ref, src_ref, bdst_ref, bound_ref, own_up_ref, own_down_ref, low_ref,
    high_ref,
    q_ref, rows_ref, dqb_ref, back_ref,
):
    high, low = two(emb_ref[...])
    pick = ones(hits(ROWS, src_ref[...]))
    rows = mm(high, pick, NN) + mm(low, pick, NN)
    rows_ref[...] = rows
    columns = weights(relw_ref[...], tile_numbers(info_ref[:1, :]))
    q_ref[:, :E_ROWS] = scaled(rows, columns).astype(BF)
    qb = own_up_ref[:D, BND:]
    q_ref[:, E_ROWS:] = qb
    near = jnp.concatenate([low_ref[:D, :BND], high_ref[:D, :BND]], axis=1)
    first, second = two(pull(mm(near, qb, TN), hits(2 * BND, bdst_ref[...])))
    dqb_ref[...] = mm(near, first, NN) + mm(near, second, NN)
    grads = []
    for got_ref, mine_ref, shift in ((low_ref, own_down_ref, BND), (high_ref, own_up_ref, 0)):
        qn = got_ref[:D, BND:]
        ids = got_ref[D:, :].astype(F32)[:1, :B_ROWS].astype(jnp.int32) - shift
        first, second = two(pull(mm(mine_ref[:D, :BND], qn, TN), hits(BND, ids)))
        grads.append(mm(qn, first, NT) + mm(qn, second, NT))
    first, second = two(jnp.concatenate(grads, axis=1))
    pick = ones(hits(ROWS, bound_ref[...]))
    back_ref[...] = mm(first, pick, NT) + mm(second, pick, NT)


def coefficients(scores, dst, live, second):
    edge = lax.broadcasted_iota(jnp.int32, (1, A_ROWS), 1)
    valid = jnp.where((edge < live * TILE) | (edge >= E_ROWS), 1.0, 0.0)
    counts = jnp.where(
        lax.broadcasted_iota(jnp.int32, (ROWS, 1), 0) < TILE, NEG_TILES - second, second
    )
    dneg = (jax.nn.sigmoid(scores) * (valid / NEG)).astype(BF).astype(F32) * counts
    positive = pull(scores[:, :E_ROWS], hits(ROWS, dst)) * valid[:, :E_ROWS]
    high, low = two(dneg[:, :E_ROWS] + positive)
    return jnp.concatenate([high, dneg[:, E_ROWS:].astype(BF)], axis=1), low


def relation_kernel(
    info_ref, got_ref, other_ref, q_ref, rows_ref, brows_ref, dqb_ref, relw_ref, dst_ref,
    gw_ref, step_ref,
):
    info = info_ref[:1, :]
    ids = tile_numbers(info)
    far = same_order(number(info, A_TILES + 2), got_ref[:D, :], other_ref[:D, :])
    scores = mm(far, q_ref[...], TN)
    coef, rest = coefficients(
        scores, dst_ref[...], number(info, A_TILES), info[:, A_TILES + 1 : A_TILES + 2]
    )
    chosen = relations(ids)
    dq = mm(far, coef, NN)
    dq_edge = dq[:, :E_ROWS] + mm(far, rest, NN)
    dq_band = dq[:, E_ROWS:] + dqb_ref[...]
    first = (dq_edge * rows_ref[...]).astype(BF)
    second = (dq_band * brows_ref[...]).astype(BF)
    gw = mm(chosen[:, :E_ROWS], first, NT) + mm(chosen[:, E_ROWS:], second, NT)
    gw = gw.astype(BF)
    for k in range(FIRST):
        gw_ref[k, :, :] = gw
    columns = weights(relw_ref[...], ids)
    step_ref[:, :E_ROWS] = scaled(dq_edge, columns).astype(BF)
    step_ref[:, E_ROWS:] = scaled(dq_band, columns[:, E_TILES:A_TILES]).astype(BF)


def partner_kernel(
    info_ref, got_ref, other_ref, emb_ref, relw_ref, step_ref, src_ref, bsrc_ref, back_ref,
    keep_ref, give_ref,
):
    core = number(info_ref[:1, :], A_TILES + 2)
    far = same_order(core, got_ref[:D, :], other_ref[:D, :])
    info = got_ref[D:, :].astype(F32)
    ids = jnp.concatenate([info[k : k + 1, :] for k in range(10)], axis=1).astype(jnp.int32)
    scalars = info[10:11, :]
    columns = weights(relw_ref[...], tile_numbers(scalars))
    q = scaled(mm(far, ones(hits(ROWS, ids[:, :A_ROWS])), NN), columns).astype(BF)
    scores = mm(emb_ref[...].astype(BF), q, TN)
    coef, rest = coefficients(
        scores, ids[:, A_ROWS:], number(scalars, A_TILES), scalars[:, A_TILES + 1 : A_TILES + 2]
    )
    pick = jnp.concatenate([ones(hits(ROWS, src_ref[...])), ones(hits(ROWS, bsrc_ref[...]))], axis=1)
    total = back_ref[...] + mm(step_ref[...], pick, NT) + mm(q, coef, NT)
    total = total + mm(q[:, :E_ROWS], rest, NT)
    keep_ref[...] = jnp.where(core == 0, total[:, :HALF], total[:, HALF:])
    give_ref[...] = jnp.where(core == 0, total[:, HALF:], total[:, :HALF]).astype(BF)


def final_kernel(info_ref, mine_ref, other_ref, emb_ref, state_ref, new_ref, fresh_ref):
    grad = same_order(number(info_ref[:1, :], A_TILES + 2), mine_ref[...], other_ref[...])
    fresh = state_ref[...] + jnp.sum(grad * grad, axis=0, keepdims=True) / D
    fresh_ref[...] = fresh
    new_ref[...] = emb_ref[...] - step_rate * grad / jnp.sqrt(fresh)


def swap(axes, size, number, work):
    def branch(k):
        def run(moved, *args):
            if k:
                moved = lax.ppermute(moved, axes, [(i, i ^ k) for i in range(size)])
            return (moved, *work(*args))

        return run

    return lambda *args: lax.switch(number, [branch(k) for k in range(size)], *args)


def trade(values, bit):
    return lax.ppermute(values, "rel", [(i, i ^ bit) for i in range(N_REL)])


def body(
    emb, emb_state, rel_weight, rel_state, swap_mask, src_rows, dst_rows, tile_rel, live_tiles,
    neg_tiles, bound_rows, band_src, band_dst, band_rel,
):
    mask = swap_mask[0]
    bound = bound_rows.reshape(1, 2 * BND)
    core = lax.bitwise_and(lax.axis_index("rel").astype(jnp.int32), 1).reshape(1)
    count = lax.axis_size(DOM)
    emb_t = emb.T
    part, to_up, to_down, band_rows, info = call(
        start_kernel,
        "sssssvvvvvvv",
        [
            ((SENT, HALF), BF),
            ((RIM, RIM_WIDTH), BF),
            ((RIM, RIM_WIDTH), BF),
            ((D, B_ROWS), F32),
            ((RELS, TILE), F32),
        ],
        core, tile_rel, band_rel, live_tiles, neg_tiles, emb_t, rel_weight, src_rows, dst_rows,
        band_src, band_dst, bound, limit=WIDE,
    )
    from_low = lax.ppermute(to_up, DOM, [(i, i + 1) for i in range(count - 1)])
    from_high = lax.ppermute(to_down, DOM, [(i + 1, i) for i in range(count - 1)])
    (got,) = swap(XY, 8, lax.shift_right_logical(mask, 4), lambda: ())(part)

    def sources(*args):
        return call(
            source_kernel,
            "vvvvvvvvvv",
            [((D, A_ROWS), BF), ((D, E_ROWS), F32), ((D, B_ROWS), F32), ((D, ROWS), F32)],
            *args, limit=WIDE,
        )

    along_z = swap(ZZ, Z, lax.bitwise_and(mask, 15), sources)
    got, q, rows, dq_band, back = along_z(
        got, info, emb_t, rel_weight, src_rows, band_dst, bound, to_up, to_down, from_low, from_high
    )
    other_half = trade(got, 1)
    gw, step = call(
        relation_kernel,
        "vvvvvvvvv",
        [((FIRST, RELS, D), BF), ((D, A_ROWS), BF)],
        info, got, other_half, q, rows, band_rows, dq_band, rel_weight, dst_rows,
    )
    gw = lax.all_to_all(gw, ZZ, split_axis=0, concat_axis=0, tiled=True)
    keep, give = call(
        partner_kernel,
        "vvvvvvvvv",
        [((D, HALF), F32), ((D, HALF), BF)],
        info, got, other_half, emb_t, rel_weight, step, src_rows, band_src, back,
    )
    half = (keep + trade(give, 1).astype(F32)).astype(BF)
    mine = half.astype(F32) + trade(half, 2).astype(F32)
    other = trade(mine, 1)
    new_t, fresh = call(
        final_kernel,
        "vvvvv",
        [((D, ROWS), F32), ((1, ROWS), F32)],
        info, mine, other, emb_t, emb_state.reshape(1, ROWS),
    )
    gw = jnp.sum(gw.astype(F32), axis=0).astype(BF)
    gw = jnp.broadcast_to(gw[None], (SECOND, RELS, D))
    gw = lax.all_to_all(gw, XY, split_axis=0, concat_axis=0, tiled=True)
    gw = jnp.sum(gw.astype(F32), axis=0)
    rel_new = rel_weight - step_rate * gw / jnp.sqrt(rel_state + jnp.mean(gw * gw, axis=1))[:, None]
    return (new_t.T, fresh.reshape(ROWS), rel_new)


def solution(mesh):
    fine = Mesh(mesh.devices.reshape(4, 2, 8, 2, N_REL), (*DOM, "rel"))
    in_specs = (
        P(DOM, None),
        P(DOM),
        P("rel", None),
        P("rel"),
        P(),
        P("rel", DOM),
        P("rel", DOM),
        P("rel", DOM),
        P("rel", DOM),
        P("rel", DOM),
        P(DOM),
        P("rel", DOM),
        P("rel", DOM),
        P("rel", DOM),
    )
    out_specs = (P(DOM, None), P(DOM), P("rel", None))
    return jax.shard_map(
        body, mesh=fine, in_specs=in_specs, out_specs=out_specs, check_vma=False
    )
```

```python
import jax
import jax.numpy as jnp
from jax import lax
from jax.experimental import pallas as pl
from jax.experimental.pallas import tpu as pltpu
from jax.sharding import Mesh
from jax.sharding import PartitionSpec as P

step_rate = 0.25

D = 400
TILE = 128
ROWS = 256
HALF = ROWS // 2
BND = 128
E_ROWS = 512
B_ROWS = 256
A_ROWS = E_ROWS + B_ROWS
E_TILES = E_ROWS // TILE
B_TILES = B_ROWS // TILE
A_TILES = E_TILES + B_TILES
N_REL = 4
RELS = 8
NEG_TILES = 8
NEG = NEG_TILES * TILE
INFO = 16
SENT = D + INFO
RIM_INFO = 8
RIM = D + RIM_INFO
RIM_WIDTH = BND + B_ROWS

LIMIT = 24 << 20
WIDE = 56 << 20

BF = jnp.bfloat16
F32 = jnp.float32
XY = ("x", "yh")
ZZ = ("zh", "zl")
DOM = (*XY, *ZZ)
Z = 16
FIRST = 16
SECOND = 8


def vmem():
    return pl.BlockSpec(memory_space=pltpu.VMEM)


def smem():
    return pl.BlockSpec(memory_space=pltpu.SMEM)


def call(kernel, ins, outs, *args, limit=LIMIT):
    return pl.pallas_call(
        kernel,
        in_specs=[smem() if kind == "s" else vmem() for kind in ins],
        out_specs=[vmem() for _ in outs],
        out_shape=[jax.ShapeDtypeStruct(shape, dtype) for shape, dtype in outs],
        compiler_params=pltpu.CompilerParams(vmem_limit_bytes=limit),
    )(*args)


def mm(a, b, dims):
    return lax.dot_general(a, b, (dims, ((), ())), preferred_element_type=F32)


NN = ((1,), (0,))
NT = ((1,), (1,))
TN = ((0,), (0,))


def two(values):
    high = values.astype(BF)
    return high, (values - high.astype(F32)).astype(BF)


def hits(count, ids):
    return lax.broadcasted_iota(jnp.int32, (count, ids.shape[1]), 0) == ids


def ones(mask):
    return mask.astype(F32).astype(BF)


def stacked(count, width, lists):
    row = lax.broadcasted_iota(jnp.int32, (count, width), 0)
    block = jnp.zeros((count, width), F32)
    for k, values in enumerate(lists):
        values = values.astype(F32)
        if values.shape[1] < width:
            values = jnp.concatenate(
                [values, jnp.zeros((1, width - values.shape[1]), F32)], axis=1
            )
        block = jnp.where(row == k, values, block)
    return block


def relations(ids):
    spread = [jnp.broadcast_to(ident, (1, TILE)).astype(jnp.int32) for ident in ids]
    return ones(hits(RELS, jnp.concatenate(spread, axis=1)))


def weights(relw, ids):
    lane = lax.broadcasted_iota(jnp.int32, (RELS, TILE), 1)
    row = lax.broadcasted_iota(jnp.int32, (RELS, TILE), 0)
    chosen = jnp.zeros((RELS, TILE), F32)
    for t, ident in enumerate(ids):
        chosen = jnp.where((lane == t) & (row == ident), 1.0, chosen)
    chosen = chosen.astype(BF)
    high = relw.astype(BF)
    rest = relw - high.astype(F32)
    middle = rest.astype(BF)
    low = (rest - middle.astype(F32)).astype(BF)
    return (mm(high, chosen, TN) + mm(middle, chosen, TN)) + mm(low, chosen, TN)


def scaled(rows, columns):
    return jnp.concatenate(
        [
            rows[:, t * TILE : (t + 1) * TILE] * columns[:, t : t + 1]
            for t in range(rows.shape[1] // TILE)
        ],
        axis=1,
    )


def number(info, k):
    return info[:, k : k + 1].astype(jnp.int32)


def tile_numbers(info):
    return [number(info, k) for k in range(A_TILES)]


def parts_of(info):
    ids = jnp.concatenate([info[k : k + 1, :] for k in range(10)], axis=1).astype(jnp.int32)
    return ids[:, :A_ROWS], ids[:, A_ROWS:], info[10:11, :]


def same_order(core, own, other):
    first = core == 0
    return jnp.concatenate([jnp.where(first, own, other), jnp.where(first, other, own)], axis=1)


def start_kernel(
    core_ref, tile_ref, band_ref, live_ref, neg_ref, emb_ref, relw_ref, src_ref, dst_ref, bsrc_ref,
    bdst_ref, bound_ref,
    part_ref, up_ref, down_ref, brows_ref, info_ref,
):
    high, low = two(emb_ref[...])
    part_ref[:D, :] = jnp.where(core_ref[0] == 0, high[:, :HALF], high[:, HALF:])
    numbers = [tile_ref[0, t] for t in range(E_TILES)] + [band_ref[0, t] for t in range(B_TILES)]
    second = neg_ref[0, 0]
    for t in range(1, NEG_TILES):
        second = second + neg_ref[0, t]
    lane = lax.broadcasted_iota(jnp.int32, (1, TILE), 1)
    scalars = jnp.zeros((1, TILE), F32)
    for k, value in enumerate([*numbers, live_ref[0, 0], second, core_ref[0]]):
        scalars = jnp.where(lane == k, value.astype(F32), scalars)
    lists = []
    for ref in (src_ref, bsrc_ref, dst_ref):
        lists += [ref[:, k : k + TILE] for k in range(0, ref.shape[1], TILE)]
    info = stacked(INFO, TILE, [*lists, scalars])
    info_ref[...] = info
    part_ref[D:, :] = info.astype(BF)
    rim = mm(high, ones(hits(ROWS, bound_ref[...])), NN).astype(BF)
    up_ref[:D, :BND] = rim[:, BND:]
    down_ref[:D, :BND] = rim[:, :BND]
    pick = ones(hits(ROWS, bsrc_ref[...]))
    rows = mm(high, pick, NN) + mm(low, pick, NN)
    brows_ref[...] = rows
    q = scaled(rows, weights(relw_ref[...], numbers[E_TILES:])).astype(BF)
    info = stacked(RIM_INFO, RIM_WIDTH, [bdst_ref[...]]).astype(BF)
    for ref in (up_ref, down_ref):
        ref[:D, BND:] = q
        ref[D:, :] = info


def pull(scores, hit):
    pos = jnp.sum(jnp.where(hit, scores, 0.0), axis=0, keepdims=True)
    return jnp.where(hit, -jax.nn.sigmoid(-pos), 0.0)


def source_kernel(
    info_ref, emb_ref, relw_ref, bdst_ref, bound_ref, own_up_ref, own_down_ref, low_ref,
    high_ref,
    q_ref, rows_ref, dqb_ref, back_ref,
):
    high, low = two(emb_ref[...])
    src, _, scalars = parts_of(info_ref[...])
    pick = ones(hits(ROWS, src[:, :E_ROWS]))
    rows = mm(high, pick, NN) + mm(low, pick, NN)
    rows_ref[...] = rows
    columns = weights(relw_ref[...], tile_numbers(scalars))
    q_ref[:, :E_ROWS] = scaled(rows, columns).astype(BF)
    qb = own_up_ref[:D, BND:]
    q_ref[:, E_ROWS:] = qb
    near = jnp.concatenate([low_ref[:D, :BND], high_ref[:D, :BND]], axis=1)
    first, second = two(pull(mm(near, qb, TN), hits(2 * BND, bdst_ref[...])))
    dqb_ref[...] = mm(near, first, NN) + mm(near, second, NN)
    grads = []
    for got_ref, mine_ref, shift in ((low_ref, own_down_ref, BND), (high_ref, own_up_ref, 0)):
        qn = got_ref[:D, BND:]
        ids = got_ref[D:, :].astype(F32)[:1, :B_ROWS].astype(jnp.int32) - shift
        first, second = two(pull(mm(mine_ref[:D, :BND], qn, TN), hits(BND, ids)))
        grads.append(mm(qn, first, NT) + mm(qn, second, NT))
    first, second = two(jnp.concatenate(grads, axis=1))
    pick = ones(hits(ROWS, bound_ref[...]))
    back_ref[...] = mm(first, pick, NT) + mm(second, pick, NT)


def coefficients(scores, dst, live, second):
    edge = lax.broadcasted_iota(jnp.int32, (1, A_ROWS), 1)
    valid = jnp.where((edge < live * TILE) | (edge >= E_ROWS), 1.0, 0.0)
    counts = jnp.where(
        lax.broadcasted_iota(jnp.int32, (ROWS, 1), 0) < TILE, NEG_TILES - second, second
    )
    dneg = (jax.nn.sigmoid(scores) * (valid / NEG)).astype(BF).astype(F32) * counts
    positive = pull(scores[:, :E_ROWS], hits(ROWS, dst)) * valid[:, :E_ROWS]
    high, low = two(dneg[:, :E_ROWS] + positive)
    return jnp.concatenate([high, dneg[:, E_ROWS:].astype(BF)], axis=1), low


def relation_kernel(
    info_ref, got_ref, other_ref, q_ref, rows_ref, brows_ref, dqb_ref, relw_ref,
    gw_ref, step_ref,
):
    _, dst, info = parts_of(info_ref[...])
    ids = tile_numbers(info)
    far = same_order(number(info, A_TILES + 2), got_ref[:D, :], other_ref[:D, :])
    scores = mm(far, q_ref[...], TN)
    coef, rest = coefficients(
        scores, dst, number(info, A_TILES), info[:, A_TILES + 1 : A_TILES + 2]
    )
    chosen = relations(ids)
    dq = mm(far, coef, NN)
    dq_edge = dq[:, :E_ROWS] + mm(far, rest, NN)
    dq_band = dq[:, E_ROWS:] + dqb_ref[...]
    first = (dq_edge * rows_ref[...]).astype(BF)
    second = (dq_band * brows_ref[...]).astype(BF)
    gw = mm(chosen[:, :E_ROWS], first, NT) + mm(chosen[:, E_ROWS:], second, NT)
    gw = gw.astype(BF)
    for k in range(FIRST):
        gw_ref[k, :, :] = gw
    columns = weights(relw_ref[...], ids)
    step_ref[:, :E_ROWS] = scaled(dq_edge, columns).astype(BF)
    step_ref[:, E_ROWS:] = scaled(dq_band, columns[:, E_TILES:A_TILES]).astype(BF)


def partner_kernel(
    info_ref, got_ref, other_ref, emb_ref, relw_ref, step_ref, back_ref,
    keep_ref, give_ref,
):
    own_src, _, own_scalars = parts_of(info_ref[...])
    core = number(own_scalars, A_TILES + 2)
    far = same_order(core, got_ref[:D, :], other_ref[:D, :])
    src, dst, scalars = parts_of(got_ref[D:, :].astype(F32))
    columns = weights(relw_ref[...], tile_numbers(scalars))
    q = scaled(mm(far, ones(hits(ROWS, src)), NN), columns).astype(BF)
    scores = mm(emb_ref[...].astype(BF), q, TN)
    coef, rest = coefficients(
        scores, dst, number(scalars, A_TILES), scalars[:, A_TILES + 1 : A_TILES + 2]
    )
    pick = ones(hits(ROWS, own_src))
    total = back_ref[...] + mm(step_ref[...], pick, NT) + mm(q, coef, NT)
    total = total + mm(q[:, :E_ROWS], rest, NT)
    keep_ref[...] = jnp.where(core == 0, total[:, :HALF], total[:, HALF:])
    give_ref[...] = jnp.where(core == 0, total[:, HALF:], total[:, :HALF]).astype(BF)


def final_kernel(info_ref, mine_ref, other_ref, emb_ref, state_ref, new_ref, fresh_ref):
    grad = same_order(number(info_ref[10:11, :], A_TILES + 2), mine_ref[...], other_ref[...])
    fresh = state_ref[...] + jnp.sum(grad * grad, axis=0, keepdims=True) / D
    fresh_ref[...] = fresh
    new_ref[...] = emb_ref[...] - step_rate * grad / jnp.sqrt(fresh)


def swap(axes, size, number, work):
    def branch(k):
        def run(moved, *args):
            if k:
                moved = lax.ppermute(moved, axes, [(i, i ^ k) for i in range(size)])
            return (moved, *work(*args))

        return run

    return lambda *args: lax.switch(number, [branch(k) for k in range(size)], *args)


def trade(values, bit):
    return lax.ppermute(values, "rel", [(i, i ^ bit) for i in range(N_REL)])


def body(
    emb, emb_state, rel_weight, rel_state, swap_mask, src_rows, dst_rows, tile_rel, live_tiles,
    neg_tiles, bound_rows, band_src, band_dst, band_rel,
):
    mask = swap_mask[0]
    bound = bound_rows.reshape(1, 2 * BND)
    core = lax.bitwise_and(lax.axis_index("rel").astype(jnp.int32), 1).reshape(1)
    count = lax.axis_size(DOM)
    emb_t = emb.T
    part, to_up, to_down, band_rows, info = call(
        start_kernel,
        "sssssvvvvvvv",
        [
            ((SENT, HALF), BF),
            ((RIM, RIM_WIDTH), BF),
            ((RIM, RIM_WIDTH), BF),
            ((D, B_ROWS), F32),
            ((INFO, TILE), F32),
        ],
        core, tile_rel, band_rel, live_tiles, neg_tiles, emb_t, rel_weight, src_rows, dst_rows,
        band_src, band_dst, bound, limit=WIDE,
    )
    from_low = lax.ppermute(to_up, DOM, [(i, i + 1) for i in range(count - 1)])
    from_high = lax.ppermute(to_down, DOM, [(i + 1, i) for i in range(count - 1)])
    (got,) = swap(XY, 8, lax.shift_right_logical(mask, 4), lambda: ())(part)

    def sources(*args):
        return call(
            source_kernel,
            "vvvvvvvvv",
            [((D, A_ROWS), BF), ((D, E_ROWS), F32), ((D, B_ROWS), F32), ((D, ROWS), F32)],
            *args, limit=WIDE,
        )

    along_z = swap(ZZ, Z, lax.bitwise_and(mask, 15), sources)
    got, q, rows, dq_band, back = along_z(
        got, info, emb_t, rel_weight, band_dst, bound, to_up, to_down, from_low, from_high
    )
    other_half = trade(got, 1)
    gw, step = call(
        relation_kernel,
        "vvvvvvvv",
        [((FIRST, RELS, D), BF), ((D, A_ROWS), BF)],
        info, got, other_half, q, rows, band_rows, dq_band, rel_weight,
    )
    gw = lax.all_to_all(gw, ZZ, split_axis=0, concat_axis=0, tiled=True)
    keep, give = call(
        partner_kernel,
        "vvvvvvv",
        [((D, HALF), F32), ((D, HALF), BF)],
        info, got, other_half, emb_t, rel_weight, step, back,
    )
    half = (keep + trade(give, 1).astype(F32)).astype(BF)
    mine = half.astype(F32) + trade(half, 2).astype(F32)
    other = trade(mine, 1)
    new_t, fresh = call(
        final_kernel,
        "vvvvv",
        [((D, ROWS), F32), ((1, ROWS), F32)],
        info, mine, other, emb_t, emb_state.reshape(1, ROWS),
    )
    gw = jnp.sum(gw.astype(F32), axis=0).astype(BF)
    gw = jnp.broadcast_to(gw[None], (SECOND, RELS, D))
    gw = lax.all_to_all(gw, XY, split_axis=0, concat_axis=0, tiled=True)
    gw = jnp.sum(gw.astype(F32), axis=0)
    rel_new = rel_weight - step_rate * gw / jnp.sqrt(rel_state + jnp.mean(gw * gw, axis=1))[:, None]
    return (new_t.T, fresh.reshape(ROWS), rel_new)


def solution(mesh):
    fine = Mesh(mesh.devices.reshape(4, 2, 8, 2, N_REL), (*DOM, "rel"))
    in_specs = (
        P(DOM, None),
        P(DOM),
        P("rel", None),
        P("rel"),
        P(),
        P("rel", DOM),
        P("rel", DOM),
        P("rel", DOM),
        P("rel", DOM),
        P("rel", DOM),
        P(DOM),
        P("rel", DOM),
        P("rel", DOM),
        P("rel", DOM),
    )
    out_specs = (P(DOM, None), P(DOM), P("rel", None))
    return jax.shard_map(
        body, mesh=fine, in_specs=in_specs, out_specs=out_specs, check_vma=False
    )
```

```python
import jax
import jax.numpy as jnp
from jax import lax
from jax.experimental import pallas as pl
from jax.experimental.pallas import tpu as pltpu
from jax.sharding import Mesh
from jax.sharding import PartitionSpec as P

step_rate = 0.25

D = 400
TILE = 128
ROWS = 256
HALF = ROWS // 2
BND = 128
E_ROWS = 512
B_ROWS = 256
A_ROWS = E_ROWS + B_ROWS
E_TILES = E_ROWS // TILE
B_TILES = B_ROWS // TILE
A_TILES = E_TILES + B_TILES
N_REL = 4
RELS = 8
NEG_TILES = 8
NEG = NEG_TILES * TILE
INFO = 16
SENT = D + INFO
RIM_INFO = 8
RIM = D + RIM_INFO
RIM_WIDTH = BND + B_ROWS

LIMIT = 24 << 20
WIDE = 56 << 20

BF = jnp.bfloat16
F32 = jnp.float32
XY = ("x", "yh")
ZZ = ("zh", "zl")
DOM = (*XY, *ZZ)
Z = 16
FIRST = 16
SECOND = 8


def vmem():
    return pl.BlockSpec(memory_space=pltpu.VMEM)


def smem():
    return pl.BlockSpec(memory_space=pltpu.SMEM)


def call(kernel, ins, outs, *args, limit=LIMIT):
    return pl.pallas_call(
        kernel,
        in_specs=[smem() if kind == "s" else vmem() for kind in ins],
        out_specs=[vmem() for _ in outs],
        out_shape=[jax.ShapeDtypeStruct(shape, dtype) for shape, dtype in outs],
        compiler_params=pltpu.CompilerParams(vmem_limit_bytes=limit),
    )(*args)


def mm(a, b, dims):
    return lax.dot_general(a, b, (dims, ((), ())), preferred_element_type=F32)


NN = ((1,), (0,))
NT = ((1,), (1,))
TN = ((0,), (0,))


def two(values):
    high = values.astype(BF)
    return high, (values - high.astype(F32)).astype(BF)


def hits(count, ids):
    return lax.broadcasted_iota(jnp.int32, (count, ids.shape[1]), 0) == ids


def ones(mask):
    return mask.astype(F32).astype(BF)


def stacked(count, width, lists):
    row = lax.broadcasted_iota(jnp.int32, (count, width), 0)
    block = jnp.zeros((count, width), F32)
    for k, values in enumerate(lists):
        values = values.astype(F32)
        if values.shape[1] < width:
            values = jnp.concatenate(
                [values, jnp.zeros((1, width - values.shape[1]), F32)], axis=1
            )
        block = jnp.where(row == k, values, block)
    return block


def relations(ids):
    spread = [jnp.broadcast_to(ident, (1, TILE)).astype(jnp.int32) for ident in ids]
    return ones(hits(RELS, jnp.concatenate(spread, axis=1)))


def weights(relw, ids):
    lane = lax.broadcasted_iota(jnp.int32, (RELS, TILE), 1)
    row = lax.broadcasted_iota(jnp.int32, (RELS, TILE), 0)
    chosen = jnp.zeros((RELS, TILE), F32)
    for t, ident in enumerate(ids):
        chosen = jnp.where((lane == t) & (row == ident), 1.0, chosen)
    chosen = chosen.astype(BF)
    high = relw.astype(BF)
    rest = relw - high.astype(F32)
    middle = rest.astype(BF)
    low = (rest - middle.astype(F32)).astype(BF)
    return (mm(high, chosen, TN) + mm(middle, chosen, TN)) + mm(low, chosen, TN)


def scaled(rows, columns):
    return jnp.concatenate(
        [
            rows[:, t * TILE : (t + 1) * TILE] * columns[:, t : t + 1]
            for t in range(rows.shape[1] // TILE)
        ],
        axis=1,
    )


def number(info, k):
    return info[:, k : k + 1].astype(jnp.int32)


def tile_numbers(info):
    return [number(info, k) for k in range(A_TILES)]


def parts_of(info):
    ids = jnp.concatenate([info[k : k + 1, :] for k in range(10)], axis=1).astype(jnp.int32)
    return ids[:, :A_ROWS], ids[:, A_ROWS:], info[10:11, :]


def same_order(core, own, other):
    first = core == 0
    return jnp.concatenate([jnp.where(first, own, other), jnp.where(first, other, own)], axis=1)


def start_kernel(
    core_ref, tile_ref, band_ref, live_ref, neg_ref, emb_ref, relw_ref, src_ref, dst_ref, bsrc_ref,
    bdst_ref, bound_ref,
    part_ref, up_ref, down_ref, brows_ref, info_ref,
):
    high, low = two(emb_ref[...])
    part_ref[:D, :] = jnp.where(core_ref[0] == 0, high[:, :HALF], high[:, HALF:])
    numbers = [tile_ref[0, t] for t in range(E_TILES)] + [band_ref[0, t] for t in range(B_TILES)]
    second = neg_ref[0, 0]
    for t in range(1, NEG_TILES):
        second = second + neg_ref[0, t]
    lane = lax.broadcasted_iota(jnp.int32, (1, TILE), 1)
    scalars = jnp.zeros((1, TILE), F32)
    for k, value in enumerate([*numbers, live_ref[0, 0], second, core_ref[0]]):
        scalars = jnp.where(lane == k, value.astype(F32), scalars)
    lists = []
    for ref in (src_ref, bsrc_ref, dst_ref):
        lists += [ref[:, k : k + TILE] for k in range(0, ref.shape[1], TILE)]
    info = stacked(INFO, TILE, [*lists, scalars])
    info_ref[...] = info
    part_ref[D:, :] = info.astype(BF)
    rim = mm(high, ones(hits(ROWS, bound_ref[...])), NN).astype(BF)
    up_ref[:D, :BND] = rim[:, BND:]
    down_ref[:D, :BND] = rim[:, :BND]
    pick = ones(hits(ROWS, bsrc_ref[...]))
    rows = mm(high, pick, NN) + mm(low, pick, NN)
    brows_ref[...] = rows
    q = scaled(rows, weights(relw_ref[...], numbers[E_TILES:])).astype(BF)
    info = stacked(RIM_INFO, RIM_WIDTH, [bdst_ref[...]]).astype(BF)
    for ref in (up_ref, down_ref):
        ref[:D, BND:] = q
        ref[D:, :] = info


def pull(scores, hit):
    pos = jnp.sum(jnp.where(hit, scores, 0.0), axis=0, keepdims=True)
    return jnp.where(hit, -jax.nn.sigmoid(-pos), 0.0)


def source_kernel(
    info_ref, emb_ref, relw_ref, bdst_ref, bound_ref, own_up_ref, own_down_ref, low_ref,
    high_ref,
    q_ref, rows_ref, dqb_ref, back_ref,
):
    high, low = two(emb_ref[...])
    src, _, scalars = parts_of(info_ref[...])
    pick = ones(hits(ROWS, src[:, :E_ROWS]))
    rows = mm(high, pick, NN) + mm(low, pick, NN)
    rows_ref[...] = rows
    columns = weights(relw_ref[...], tile_numbers(scalars))
    q_ref[:, :E_ROWS] = scaled(rows, columns).astype(BF)
    qb = own_up_ref[:D, BND:]
    q_ref[:, E_ROWS:] = qb
    near = jnp.concatenate([low_ref[:D, :BND], high_ref[:D, :BND]], axis=1)
    first, second = two(pull(mm(near, qb, TN), hits(2 * BND, bdst_ref[...])))
    dqb_ref[...] = mm(near, first, NN) + mm(near, second, NN)
    grads = []
    for got_ref, mine_ref, shift in ((low_ref, own_down_ref, BND), (high_ref, own_up_ref, 0)):
        qn = got_ref[:D, BND:]
        ids = got_ref[D:, :].astype(F32)[:1, :B_ROWS].astype(jnp.int32) - shift
        first, second = two(pull(mm(mine_ref[:D, :BND], qn, TN), hits(BND, ids)))
        grads.append(mm(qn, first, NT) + mm(qn, second, NT))
    first, second = two(jnp.concatenate(grads, axis=1))
    pick = ones(hits(ROWS, bound_ref[...]))
    back_ref[...] = mm(first, pick, NT) + mm(second, pick, NT)


def coefficients(scores, dst, live, second):
    edge = lax.broadcasted_iota(jnp.int32, (1, A_ROWS), 1)
    valid = jnp.where((edge < live * TILE) | (edge >= E_ROWS), 1.0, 0.0)
    counts = jnp.where(
        lax.broadcasted_iota(jnp.int32, (ROWS, 1), 0) < TILE, NEG_TILES - second, second
    )
    dneg = (jax.nn.sigmoid(scores) * (valid / NEG)).astype(BF).astype(F32) * counts
    positive = pull(scores[:, :E_ROWS], hits(ROWS, dst)) * valid[:, :E_ROWS]
    high, low = two(dneg[:, :E_ROWS] + positive)
    return jnp.concatenate([high, dneg[:, E_ROWS:].astype(BF)], axis=1), low


def relation_kernel(
    info_ref, got_ref, other_ref, q_ref, rows_ref, brows_ref, dqb_ref, relw_ref,
    gw_ref, step_ref,
):
    _, dst, info = parts_of(info_ref[...])
    ids = tile_numbers(info)
    far = same_order(number(info, A_TILES + 2), got_ref[:D, :], other_ref[:D, :])
    scores = mm(far, q_ref[...], TN)
    coef, rest = coefficients(
        scores, dst, number(info, A_TILES), info[:, A_TILES + 1 : A_TILES + 2]
    )
    chosen = relations(ids)
    dq = mm(far, coef, NN)
    dq_edge = dq[:, :E_ROWS] + mm(far, rest, NN)
    dq_band = dq[:, E_ROWS:] + dqb_ref[...]
    first = (dq_edge * rows_ref[...]).astype(BF)
    second = (dq_band * brows_ref[...]).astype(BF)
    gw = mm(chosen[:, :E_ROWS], first, NT) + mm(chosen[:, E_ROWS:], second, NT)
    gw = gw.astype(BF)
    for k in range(FIRST):
        gw_ref[k, :, :] = gw
    columns = weights(relw_ref[...], ids)
    step_ref[:, :E_ROWS] = scaled(dq_edge, columns).astype(BF)
    step_ref[:, E_ROWS:] = scaled(dq_band, columns[:, E_TILES:A_TILES]).astype(BF)


def partner_kernel(
    info_ref, got_ref, other_ref, emb_ref, relw_ref, step_ref, back_ref,
    keep_ref, give_ref,
):
    own_src, _, own_scalars = parts_of(info_ref[...])
    core = number(own_scalars, A_TILES + 2)
    far = same_order(core, got_ref[:D, :], other_ref[:D, :])
    src, dst, scalars = parts_of(got_ref[D:, :].astype(F32))
    columns = weights(relw_ref[...], tile_numbers(scalars))
    q = scaled(mm(far, ones(hits(ROWS, src)), NN), columns).astype(BF)
    scores = mm(emb_ref[...].astype(BF), q, TN)
    coef, rest = coefficients(
        scores, dst, number(scalars, A_TILES), scalars[:, A_TILES + 1 : A_TILES + 2]
    )
    pick = ones(hits(ROWS, own_src))
    total = back_ref[...] + mm(step_ref[...], pick, NT) + mm(q, coef, NT)
    total = total + mm(q[:, :E_ROWS], rest, NT)
    keep_ref[...] = jnp.where(core == 0, total[:, :HALF], total[:, HALF:])
    give_ref[...] = jnp.where(core == 0, total[:, HALF:], total[:, :HALF]).astype(BF)


def final_kernel(info_ref, mine_ref, other_ref, emb_ref, state_ref, new_ref, fresh_ref):
    grad = same_order(number(info_ref[10:11, :], A_TILES + 2), mine_ref[...], other_ref[...])
    fresh = state_ref[...] + jnp.sum(grad * grad, axis=0, keepdims=True) / D
    fresh_ref[...] = fresh
    new_ref[...] = emb_ref[...] - step_rate * grad / jnp.sqrt(fresh)


def update_kernel(state_ref, gw_ref, relw_ref, new_ref):
    gw = gw_ref[0, :, :].astype(F32)
    for k in range(1, SECOND):
        gw = gw + gw_ref[k, :, :].astype(F32)
    row = lax.broadcasted_iota(jnp.int32, (RELS, 1), 0)
    state = jnp.zeros((RELS, 1), F32)
    for k in range(RELS):
        state = jnp.where(row == k, state_ref[k], state)
    fresh = state + jnp.sum(gw * gw, axis=1, keepdims=True) / D
    new_ref[...] = relw_ref[...] - step_rate * gw / jnp.sqrt(fresh)


def swap(axes, size, number, work):
    def branch(k):
        def run(moved, *args):
            if k:
                moved = lax.ppermute(moved, axes, [(i, i ^ k) for i in range(size)])
            return (moved, *work(*args))

        return run

    return lambda *args: lax.switch(number, [branch(k) for k in range(size)], *args)


def trade(values, bit):
    return lax.ppermute(values, "rel", [(i, i ^ bit) for i in range(N_REL)])


def body(
    emb, emb_state, rel_weight, rel_state, swap_mask, src_rows, dst_rows, tile_rel, live_tiles,
    neg_tiles, bound_rows, band_src, band_dst, band_rel,
):
    mask = swap_mask[0]
    bound = bound_rows.reshape(1, 2 * BND)
    core = lax.bitwise_and(lax.axis_index("rel").astype(jnp.int32), 1).reshape(1)
    count = lax.axis_size(DOM)
    emb_t = emb.T
    part, to_up, to_down, band_rows, info = call(
        start_kernel,
        "sssssvvvvvvv",
        [
            ((SENT, HALF), BF),
            ((RIM, RIM_WIDTH), BF),
            ((RIM, RIM_WIDTH), BF),
            ((D, B_ROWS), F32),
            ((INFO, TILE), F32),
        ],
        core, tile_rel, band_rel, live_tiles, neg_tiles, emb_t, rel_weight, src_rows, dst_rows,
        band_src, band_dst, bound, limit=WIDE,
    )
    from_low = lax.ppermute(to_up, DOM, [(i, i + 1) for i in range(count - 1)])
    from_high = lax.ppermute(to_down, DOM, [(i + 1, i) for i in range(count - 1)])
    (got,) = swap(XY, 8, lax.shift_right_logical(mask, 4), lambda: ())(part)

    def sources(*args):
        return call(
            source_kernel,
            "vvvvvvvvv",
            [((D, A_ROWS), BF), ((D, E_ROWS), F32), ((D, B_ROWS), F32), ((D, ROWS), F32)],
            *args, limit=WIDE,
        )

    along_z = swap(ZZ, Z, lax.bitwise_and(mask, 15), sources)
    got, q, rows, dq_band, back = along_z(
        got, info, emb_t, rel_weight, band_dst, bound, to_up, to_down, from_low, from_high
    )
    other_half = trade(got, 1)
    gw, step = call(
        relation_kernel,
        "vvvvvvvv",
        [((FIRST, RELS, D), BF), ((D, A_ROWS), BF)],
        info, got, other_half, q, rows, band_rows, dq_band, rel_weight,
    )
    gw = lax.all_to_all(gw, ZZ, split_axis=0, concat_axis=0, tiled=True)
    keep, give = call(
        partner_kernel,
        "vvvvvvv",
        [((D, HALF), F32), ((D, HALF), BF)],
        info, got, other_half, emb_t, rel_weight, step, back,
    )
    half = (keep + trade(give, 1).astype(F32)).astype(BF)
    mine = half.astype(F32) + trade(half, 2).astype(F32)
    other = trade(mine, 1)
    new_t, fresh = call(
        final_kernel,
        "vvvvv",
        [((D, ROWS), F32), ((1, ROWS), F32)],
        info, mine, other, emb_t, emb_state.reshape(1, ROWS),
    )
    gw = jnp.sum(gw.astype(F32), axis=0).astype(BF)
    gw = jnp.broadcast_to(gw[None], (SECOND, RELS, D))
    gw = lax.all_to_all(gw, XY, split_axis=0, concat_axis=0, tiled=True)
    (rel_new,) = call(update_kernel, "svv", [((RELS, D), F32)], rel_state, gw, rel_weight)
    return (new_t.T, fresh.reshape(ROWS), rel_new)


def solution(mesh):
    fine = Mesh(mesh.devices.reshape(4, 2, 8, 2, N_REL), (*DOM, "rel"))
    in_specs = (
        P(DOM, None),
        P(DOM),
        P("rel", None),
        P("rel"),
        P(),
        P("rel", DOM),
        P("rel", DOM),
        P("rel", DOM),
        P("rel", DOM),
        P("rel", DOM),
        P(DOM),
        P("rel", DOM),
        P("rel", DOM),
        P("rel", DOM),
    )
    out_specs = (P(DOM, None), P(DOM), P("rel", None))
    return jax.shard_map(
        body, mesh=fine, in_specs=in_specs, out_specs=out_specs, check_vma=False
    )
```
